256 devices in a mesh: row: 64 (over z, x, core), col: 4 (over y).
Axes of the slice: x: 4, y: 4, z: 8, core: 2. Of those that a mesh axis runs over, the one named last changes fastest.
Arguments:
- eigen_vectors: float32 [65536, 2048], P('row', 'col'), may hold values from -6 to 6
- panel_first: float32 [65536, 512], P('row', 'col'), may hold values from -0.0234375 to 0.0234375
- panel_second: float32 [65536, 512], P('row', 'col'), may hold values from -0.0234375 to 0.0234375
- factor_first: float32 [512, 512], replicated, as said below
- factor_second: float32 [512, 512], replicated, as said below
Outputs:
- transformed: float32 [65536, 2048], P('row', 'col')
The draws below stay inside these ranges and needn't reach their ends.
Inputs may be any that keep to these rules, and one draw needn't show every extreme that they name: factor_first is upper triangular. factor_second is upper triangular.
All inputs are finite; a program needn't handle non-finite values.
Results may differ from the reference program's by a relative error of at most 0.0001.
Values sent between devices are 32-bit elements; how exact they have to be, the bound alone decides.
A program may use at most 64 MiB of HBM per device.

```python
import math
import jax
import jax.numpy as jnp
from jax import lax

NB = 512
EIG = 2048
NROWS = 65536


def make_factor(key):
    values = jax.random.normal(key, (NB, NB), jnp.float32)
    upper_mask = jnp.triu(jnp.ones((NB, NB), jnp.float32))
    return values * upper_mask * (math.sqrt(2.0 * NROWS) / NB)


def draw_factor_first(key, part):
    return make_factor(jax.random.fold_in(key, 11))


def draw_factor_second(key, part):
    return make_factor(jax.random.fold_in(key, 23))


def steps_of(stream_key, dims, shards, low, high):
    factor_of = 1.0
    for dim, parts in shards:
        heights = jax.random.uniform(jax.random.fold_in(jax.random.fold_in(stream_key, 6), dim), (parts,), jnp.float32, low / len(shards), high / len(shards))
        factor_of = factor_of * jnp.repeat(jnp.exp(heights), dims[dim] // parts).reshape((-1,) + (1,) * (len(dims) - 1 - dim))
    return factor_of


def scatter_about(stream_key, extent, spread, most, split=(), held_as=jnp.bfloat16):
    array = jax.random.normal(stream_key, extent, jnp.float32) * spread
    if len(split) > 0:
        array = steps_of(stream_key, extent, split, -0.22, 0.18) * array
    return jnp.clip(array, min=-most, max=most).astype(held_as)


def setup_inputs(seed: int = 0) -> dict:
    keys = jax.random.split(jax.random.key(seed), 6)
    eigen_vectors = scatter_about(keys[0], (NROWS, EIG), 1.0, 6.0, ((0, 64), (1, 4)), jnp.float32)
    panel_first = scatter_about(keys[1], (NROWS, NB), NROWS ** -0.5, 0.0234375, ((0, 64), (1, 4)), jnp.float32)
    panel_second = scatter_about(keys[2], (NROWS, NB), NROWS ** -0.5, 0.0234375, ((0, 64), (1, 4)), jnp.float32)
    factor_first = draw_factor_first(jax.random.fold_in(keys[5], 71), 0)
    factor_second = draw_factor_second(jax.random.fold_in(keys[5], 71), 0)
    return dict(eigen_vectors=eigen_vectors, panel_first=panel_first, panel_second=panel_second, factor_first=factor_first, factor_second=factor_second)


def local_dot(left, right):
    return jnp.dot(left, right, precision=lax.Precision.HIGHEST, preferred_element_type=jnp.float32)


def reference(eigen_vectors, panel_first, panel_second, factor_first, factor_second):
    projected = local_dot(panel_second.T, eigen_vectors)
    after_second = eigen_vectors - local_dot(panel_second, local_dot(factor_second, projected))
    projected = local_dot(panel_first.T, after_second)
    return after_second - local_dot(panel_first, local_dot(factor_first, projected))
```

```python
import functools

import jax
import jax.numpy as jnp
from jax import lax
from jax.experimental import pallas as pl
from jax.experimental.pallas import tpu as pltpu
from jax.sharding import PartitionSpec as P


def local_dot(left, right):
    return jnp.dot(left, right, precision=lax.Precision.HIGHEST, preferred_element_type=jnp.float32)


def _allreduce_kernel(n, x_ref, o_ref, recv, rs_send, rs_recv, ag_send, ag_recv):
    me = lax.axis_index("row")
    col = lax.axis_index("col")
    h = x_ref.shape[0] // n
    mesh_id = pl.DeviceIdType.MESH

    def chunk(ref, j):
        return ref.at[pl.ds(pl.multiple_of(j * h, h), h), :]

    def rs_copy(s):
        tgt = lax.rem(me + s, n)
        return pltpu.make_async_remote_copy(
            src_ref=chunk(x_ref, tgt),
            dst_ref=recv.at[s],
            send_sem=rs_send.at[s],
            recv_sem=rs_recv.at[s],
            device_id=(tgt, col),
            device_id_type=mesh_id,
        )

    def ag_copy(s):
        tgt = lax.rem(me + s, n)
        return pltpu.make_async_remote_copy(
            src_ref=chunk(o_ref, me),
            dst_ref=chunk(o_ref, me),
            send_sem=ag_send.at[s],
            recv_sem=ag_recv.at[s],
            device_id=(tgt, col),
            device_id_type=mesh_id,
        )

    @pl.loop(1, n)
    def _(s):
        rs_copy(s).start()

    @pl.loop(1, n)
    def _(s):
        rs_copy(s).wait()

    def add(s, acc):
        return acc + recv[s]

    total = lax.fori_loop(1, n, add, x_ref[pl.ds(pl.multiple_of(me * h, h), h), :])
    o_ref[pl.ds(pl.multiple_of(me * h, h), h), :] = total

    @pl.loop(1, n)
    def _(s):
        ag_copy(s).start()

    @pl.loop(1, n)
    def _(s):
        ag_copy(s).wait()


def row_allreduce(x, n):
    rows, cols = x.shape
    h = rows // n
    return pl.pallas_call(
        functools.partial(_allreduce_kernel, n),
        out_shape=jax.ShapeDtypeStruct((rows, cols), x.dtype),
        in_specs=[pl.BlockSpec(memory_space=pltpu.VMEM)],
        out_specs=pl.BlockSpec(memory_space=pltpu.VMEM),
        scratch_shapes=[
            pltpu.VMEM((n, h, cols), x.dtype),
            pltpu.SemaphoreType.DMA((n,)),
            pltpu.SemaphoreType.DMA((n,)),
            pltpu.SemaphoreType.DMA((n,)),
            pltpu.SemaphoreType.DMA((n,)),
        ],
        compiler_params=pltpu.CompilerParams(has_side_effects=True),
        cost_estimate=pl.CostEstimate(
            flops=rows * cols, transcendentals=0, bytes_accessed=4 * rows * cols * 4
        ),
    )(x)


def on_device(n_row, eigen_vectors, panel_first, panel_second, factor_first, factor_second):
    vectors_first, vectors_second = (
        lax.all_gather(panel_first, "col", axis=1, tiled=True),
        lax.all_gather(panel_second, "col", axis=1, tiled=True),
    )
    updated = eigen_vectors
    for vectors, factor in ((vectors_second, factor_second), (vectors_first, factor_first)):
        projected = row_allreduce(local_dot(vectors.T, updated), n_row)
        updated = updated - local_dot(vectors, local_dot(factor, projected))
    return updated


def solution(mesh):
    return jax.shard_map(
        functools.partial(on_device, mesh.shape["row"]),
        mesh=mesh,
        in_specs=(P("row", "col"), P("row", "col"), P("row", "col"), P(), P()),
        out_specs=P("row", "col"),
        check_vma=False,
    )
```

```python
import functools

import jax
import jax.numpy as jnp
from jax import lax
from jax.experimental import pallas as pl
from jax.experimental.pallas import tpu as pltpu
from jax.sharding import PartitionSpec as P


def local_dot(left, right):
    return jnp.dot(left, right, precision=lax.Precision.HIGHEST, preferred_element_type=jnp.float32)


def _allreduce_kernel(groups, x_ref, o_ref, buf1, buf2, recv1, recv2, recv3, send_sems, recv_sems):
    me = lax.axis_index("row")
    col = lax.axis_index("col")
    g1, g2, g3 = groups
    s1, s2, s3 = 1, g1, g1 * g2
    i1 = lax.rem(me, g1)
    i2 = lax.rem(me // s2, g2)
    i3 = me // s3
    rows = x_ref.shape[0]
    p1 = rows // g1
    p2 = p1 // g2
    p3 = p2 // g3
    mesh_id = pl.DeviceIdType.MESH

    def rows_of(ref, start, size):
        return ref.at[pl.ds(pl.multiple_of(start, size), size), :]

    def exchange(stage, g, stride, mine, src_of, dst_of):
        def copy(s):
            j = lax.rem(mine + s, g)
            return pltpu.make_async_remote_copy(
                src_ref=src_of(j),
                dst_ref=dst_of(j, s),
                send_sem=send_sems.at[stage, s],
                recv_sem=recv_sems.at[stage, s],
                device_id=(me + (j - mine) * stride, col),
                device_id_type=mesh_id,
            )

        @pl.loop(1, g)
        def _(s):
            copy(s).start()

        @pl.loop(1, g)
        def _(s):
            copy(s).wait()

    def reduce_stage(stage, g, stride, mine, src, piece, recv):
        exchange(stage, g, stride, mine, lambda j: rows_of(src, j * piece, piece), lambda j, s: recv.at[s])
        return lax.fori_loop(1, g, lambda s, acc: acc + recv[s], src[pl.ds(pl.multiple_of(mine * piece, piece), piece), :])

    buf1[...] = reduce_stage(0, g1, s1, i1, x_ref, p1, recv1)
    buf2[...] = reduce_stage(1, g2, s2, i2, buf1, p2, recv2)
    base3 = i1 * p1 + i2 * p2
    o_ref[pl.ds(pl.multiple_of(base3 + i3 * p3, p3), p3), :] = reduce_stage(2, g3, s3, i3, buf2, p3, recv3)

    def gather_stage(stage, g, stride, mine, base, block):
        own = rows_of(o_ref, base + mine * block, block)
        exchange(stage, g, stride, mine, lambda j: own, lambda j, s: own)

    gather_stage(3, g3, s3, i3, base3, p3)
    gather_stage(4, g2, s2, i2, i1 * p1, p2)
    gather_stage(5, g1, s1, i1, 0, p1)


def row_allreduce(x, n):
    rows, cols = x.shape
    groups = (2, 4, n // 8)
    g1, g2, g3 = groups
    p1 = rows // g1
    p2 = p1 // g2
    p3 = p2 // g3
    return pl.pallas_call(
        functools.partial(_allreduce_kernel, groups),
        out_shape=jax.ShapeDtypeStruct((rows, cols), x.dtype),
        in_specs=[pl.BlockSpec(memory_space=pltpu.VMEM)],
        out_specs=pl.BlockSpec(memory_space=pltpu.VMEM),
        scratch_shapes=[
            pltpu.VMEM((p1, cols), x.dtype),
            pltpu.VMEM((p2, cols), x.dtype),
            pltpu.VMEM((g1, p1, cols), x.dtype),
            pltpu.VMEM((g2, p2, cols), x.dtype),
            pltpu.VMEM((g3, p3, cols), x.dtype),
            pltpu.SemaphoreType.DMA((6, max(groups))),
            pltpu.SemaphoreType.DMA((6, max(groups))),
        ],
        compiler_params=pltpu.CompilerParams(has_side_effects=True),
        cost_estimate=pl.CostEstimate(
            flops=rows * cols, transcendentals=0, bytes_accessed=4 * rows * cols * 4
        ),
    )(x)


def on_device(n_row, eigen_vectors, panel_first, panel_second, factor_first, factor_second):
    vectors_first, vectors_second = (
        lax.all_gather(panel_first, "col", axis=1, tiled=True),
        lax.all_gather(panel_second, "col", axis=1, tiled=True),
    )
    updated = eigen_vectors
    for vectors, factor in ((vectors_second, factor_second), (vectors_first, factor_first)):
        projected = row_allreduce(local_dot(vectors.T, updated), n_row)
        updated = updated - local_dot(vectors, local_dot(factor, projected))
    return updated


def solution(mesh):
    return jax.shard_map(
        functools.partial(on_device, mesh.shape["row"]),
        mesh=mesh,
        in_specs=(P("row", "col"), P("row", "col"), P("row", "col"), P(), P()),
        out_specs=P("row", "col"),
        check_vma=False,
    )
```

```python
import functools

import jax
import jax.numpy as jnp
from jax import lax
from jax.experimental import pallas as pl
from jax.experimental.pallas import tpu as pltpu
from jax.sharding import PartitionSpec as P


def local_dot(left, right):
    return jnp.dot(left, right, precision=lax.Precision.HIGHEST, preferred_element_type=jnp.float32)


def _allreduce_kernel(groups, x_ref, t_ref, o_ref, buf1, buf2, recv1, recv2, recv3, send_sems, recv_sems):
    me = lax.axis_index("row")
    col = lax.axis_index("col")
    g1, g2, g3 = groups
    s1, s2, s3 = 1, g1, g1 * g2
    i1 = lax.rem(me, g1)
    i2 = lax.rem(me // s2, g2)
    i3 = me // s3
    rows = x_ref.shape[0]
    p1 = rows // g1
    p2 = p1 // g2
    p3 = p2 // g3
    mesh_id = pl.DeviceIdType.MESH

    def rows_of(ref, start, size):
        return ref.at[pl.ds(pl.multiple_of(start, size), size), :]

    def exchange(stage, g, stride, mine, src_of, dst_of):
        def copy(s):
            j = lax.rem(mine + s, g)
            return pltpu.make_async_remote_copy(
                src_ref=src_of(j),
                dst_ref=dst_of(j, s),
                send_sem=send_sems.at[stage, s],
                recv_sem=recv_sems.at[stage, s],
                device_id=(me + (j - mine) * stride, col),
                device_id_type=mesh_id,
            )

        @pl.loop(1, g)
        def _(s):
            copy(s).start()

        @pl.loop(1, g)
        def _(s):
            copy(s).wait()

    def reduce_stage(stage, g, stride, mine, src, piece, recv):
        exchange(stage, g, stride, mine, lambda j: rows_of(src, j * piece, piece), lambda j, s: recv.at[s])
        return lax.fori_loop(1, g, lambda s, acc: acc + recv[s], src[pl.ds(pl.multiple_of(mine * piece, piece), piece), :])

    buf1[...] = reduce_stage(0, g1, s1, i1, x_ref, p1, recv1)
    buf2[...] = reduce_stage(1, g2, s2, i2, buf1, p2, recv2)
    base3 = i1 * p1 + i2 * p2
    reduced = reduce_stage(2, g3, s3, i3, buf2, p3, recv3)
    o_ref[pl.ds(pl.multiple_of(base3 + i3 * p3, p3), p3), :] = jnp.dot(
        reduced, t_ref[...], precision=lax.Precision.HIGHEST, preferred_element_type=jnp.float32
    )

    def gather_stage(stage, g, stride, mine, base, block):
        own = rows_of(o_ref, base + mine * block, block)
        exchange(stage, g, stride, mine, lambda j: own, lambda j, s: own)

    gather_stage(3, g3, s3, i3, base3, p3)
    gather_stage(4, g2, s2, i2, i1 * p1, p2)
    gather_stage(5, g1, s1, i1, 0, p1)


def row_allreduce_times(x, t_transposed, n):
    rows, cols = x.shape
    groups = (2, 4, n // 8)
    g1, g2, g3 = groups
    p1 = rows // g1
    p2 = p1 // g2
    p3 = p2 // g3
    return pl.pallas_call(
        functools.partial(_allreduce_kernel, groups),
        out_shape=jax.ShapeDtypeStruct((rows, cols), x.dtype),
        in_specs=[pl.BlockSpec(memory_space=pltpu.VMEM)] * 2,
        out_specs=pl.BlockSpec(memory_space=pltpu.VMEM),
        scratch_shapes=[
            pltpu.VMEM((p1, cols), x.dtype),
            pltpu.VMEM((p2, cols), x.dtype),
            pltpu.VMEM((g1, p1, cols), x.dtype),
            pltpu.VMEM((g2, p2, cols), x.dtype),
            pltpu.VMEM((g3, p3, cols), x.dtype),
            pltpu.SemaphoreType.DMA((6, max(groups))),
            pltpu.SemaphoreType.DMA((6, max(groups))),
        ],
        compiler_params=pltpu.CompilerParams(has_side_effects=True),
        cost_estimate=pl.CostEstimate(
            flops=rows * cols, transcendentals=0, bytes_accessed=4 * rows * cols * 4
        ),
    )(x, t_transposed)


def on_device(n_row, eigen_vectors, panel_first, panel_second, factor_first, factor_second):
    vectors_first, vectors_second = (
        lax.all_gather(panel_first, "col", axis=1, tiled=True),
        lax.all_gather(panel_second, "col", axis=1, tiled=True),
    )
    updated = eigen_vectors
    for vectors, factor in ((vectors_second, factor_second), (vectors_first, factor_first)):
        partial_t = lax.dot_general(updated, vectors, (((0,), (0,)), ((), ())), precision=lax.Precision.HIGHEST, preferred_element_type=jnp.float32)
        applied_t = row_allreduce_times(partial_t, factor.T, n_row)
        updated = updated - lax.dot_general(vectors, applied_t, (((1,), (1,)), ((), ())), precision=lax.Precision.HIGHEST, preferred_element_type=jnp.float32)
    return updated


def solution(mesh):
    return jax.shard_map(
        functools.partial(on_device, mesh.shape["row"]),
        mesh=mesh,
        in_specs=(P("row", "col"), P("row", "col"), P("row", "col"), P(), P()),
        out_specs=P("row", "col"),
        check_vma=False,
    )
```

```python
import functools

import jax
import jax.numpy as jnp
from jax import lax
from jax.experimental import pallas as pl
from jax.experimental.pallas import tpu as pltpu
from jax.sharding import PartitionSpec as P


def local_dot(left, right):
    return jnp.dot(left, right, precision=lax.Precision.HIGHEST, preferred_element_type=jnp.float32)


def _allreduce_kernel(groups, x_ref, t_ref, o_ref, buf1, buf2, recv1, recv2, recv3, send_sems, recv_sems):
    me = lax.axis_index("row")
    col = lax.axis_index("col")
    g1, g2, g3 = groups
    s1, s2, s3 = 1, g1, g1 * g2
    i1 = lax.rem(me, g1)
    i2 = lax.rem(me // s2, g2)
    i3 = me // s3
    rows = x_ref.shape[0]
    p1 = rows // g1
    p2 = p1 // g2
    p3 = p2 // g3
    mesh_id = pl.DeviceIdType.MESH

    def rows_of(ref, start, size):
        return ref.at[pl.ds(pl.multiple_of(start, size), size), :]

    def exchange(stage, g, stride, mine, src_of, dst_of):
        def copy(s):
            j = lax.rem(mine + s, g)
            return pltpu.make_async_remote_copy(
                src_ref=src_of(j),
                dst_ref=dst_of(j, s),
                send_sem=send_sems.at[stage, s],
                recv_sem=recv_sems.at[stage, s],
                device_id=(me + (j - mine) * stride, col),
                device_id_type=mesh_id,
            )

        @pl.loop(1, g)
        def _(s):
            copy(s).start()

        @pl.loop(1, g)
        def _(s):
            copy(s).wait()

    def reduce_stage(stage, g, stride, mine, src, piece, recv):
        exchange(stage, g, stride, mine, lambda j: rows_of(src, j * piece, piece), lambda j, s: recv.at[s])
        return lax.fori_loop(1, g, lambda s, acc: acc + recv[s], src[pl.ds(pl.multiple_of(mine * piece, piece), piece), :])

    buf1[...] = reduce_stage(0, g1, s1, i1, x_ref, p1, recv1)
    buf2[...] = reduce_stage(1, g2, s2, i2, buf1, p2, recv2)
    base3 = i1 * p1 + i2 * p2
    reduced = reduce_stage(2, g3, s3, i3, buf2, p3, recv3)
    o_ref[pl.ds(pl.multiple_of(base3 + i3 * p3, p3), p3), :] = jnp.dot(
        reduced, t_ref[...], precision=lax.Precision.HIGHEST, preferred_element_type=jnp.float32
    )

    def gather_stage(stage, g, stride, mine, base, block):
        own = rows_of(o_ref, base + mine * block, block)
        exchange(stage, g, stride, mine, lambda j: own, lambda j, s: own)

    gather_stage(3, g3, s3, i3, base3, p3)
    gather_stage(4, g2, s2, i2, i1 * p1, p2)
    gather_stage(5, g1, s1, i1, 0, p1)


def row_allreduce_times(x, t_transposed, n):
    rows, cols = x.shape
    groups = (2, 4, n // 8)
    g1, g2, g3 = groups
    p1 = rows // g1
    p2 = p1 // g2
    p3 = p2 // g3
    return pl.pallas_call(
        functools.partial(_allreduce_kernel, groups),
        out_shape=jax.ShapeDtypeStruct((rows, cols), x.dtype),
        in_specs=[pl.BlockSpec(memory_space=pltpu.VMEM)] * 2,
        out_specs=pl.BlockSpec(memory_space=pltpu.VMEM),
        scratch_shapes=[
            pltpu.VMEM((p1, cols), x.dtype),
            pltpu.VMEM((p2, cols), x.dtype),
            pltpu.VMEM((g1, p1, cols), x.dtype),
            pltpu.VMEM((g2, p2, cols), x.dtype),
            pltpu.VMEM((g3, p3, cols), x.dtype),
            pltpu.SemaphoreType.DMA((6, max(groups))),
            pltpu.SemaphoreType.DMA((6, max(groups))),
        ],
        compiler_params=pltpu.CompilerParams(has_side_effects=True),
        cost_estimate=pl.CostEstimate(
            flops=rows * cols, transcendentals=0, bytes_accessed=4 * rows * cols * 4
        ),
    )(x, t_transposed)


def _col_gather_kernel(n, v_ref, o_ref, send_sems, recv_sems):
    me = lax.axis_index("col")
    row = lax.axis_index("row")
    w = v_ref.shape[1]
    own = o_ref.at[:, pl.ds(pl.multiple_of(me * w, w), w)]

    def copy(s):
        return pltpu.make_async_remote_copy(
            src_ref=v_ref,
            dst_ref=own,
            send_sem=send_sems.at[s],
            recv_sem=recv_sems.at[s],
            device_id=(row, lax.rem(me + s, n)),
            device_id_type=pl.DeviceIdType.MESH,
        )

    @pl.loop(1, n)
    def _(s):
        copy(s).start()

    own[...] = v_ref[...]

    @pl.loop(1, n)
    def _(s):
        copy(s).wait()


def col_gather(v, n):
    rows, w = v.shape
    return pl.pallas_call(
        functools.partial(_col_gather_kernel, n),
        out_shape=jax.ShapeDtypeStruct((rows, w * n), v.dtype),
        in_specs=[pl.BlockSpec(memory_space=pltpu.VMEM)],
        out_specs=pl.BlockSpec(memory_space=pltpu.VMEM),
        scratch_shapes=[pltpu.SemaphoreType.DMA((n,)), pltpu.SemaphoreType.DMA((n,))],
        compiler_params=pltpu.CompilerParams(has_side_effects=True),
        cost_estimate=pl.CostEstimate(flops=0, transcendentals=0, bytes_accessed=2 * rows * w * n * 4),
    )(v)


def on_device(n_row, n_col, eigen_vectors, panel_first, panel_second, factor_first, factor_second):
    vectors_second = col_gather(panel_second, n_col)
    vectors_second, panel_first = lax.optimization_barrier((vectors_second, panel_first))
    vectors_first = lax.all_gather(panel_first, "col", axis=1, tiled=True)
    updated = eigen_vectors
    for vectors, factor in ((vectors_second, factor_second), (vectors_first, factor_first)):
        partial_t = lax.dot_general(updated, vectors, (((0,), (0,)), ((), ())), precision=lax.Precision.HIGHEST, preferred_element_type=jnp.float32)
        applied_t = row_allreduce_times(partial_t, factor.T, n_row)
        updated = updated - lax.dot_general(vectors, applied_t, (((1,), (1,)), ((), ())), precision=lax.Precision.HIGHEST, preferred_element_type=jnp.float32)
    return updated


def solution(mesh):
    return jax.shard_map(
        functools.partial(on_device, mesh.shape["row"], mesh.shape["col"]),
        mesh=mesh,
        in_specs=(P("row", "col"), P("row", "col"), P("row", "col"), P(), P()),
        out_specs=P("row", "col"),
        check_vma=False,
    )
```

```python
import functools

import jax
import jax.numpy as jnp
from jax import lax
from jax.experimental import pallas as pl
from jax.experimental.pallas import tpu as pltpu
from jax.sharding import PartitionSpec as P


def local_dot(left, right):
    return jnp.dot(left, right, precision=lax.Precision.HIGHEST, preferred_element_type=jnp.float32)


def _allreduce_kernel(groups, x_ref, t_ref, o_ref, buf1, buf2, recv1, recv2, recv3, send_sems, recv_sems):
    me = lax.axis_index("row")
    col = lax.axis_index("col")
    g1, g2, g3 = groups
    s1, s2, s3 = 1, g1, g1 * g2
    i1 = lax.rem(me, g1)
    i2 = lax.rem(me // s2, g2)
    i3 = me // s3
    rows = x_ref.shape[0]
    p1 = rows // g1
    p2 = p1 // g2
    p3 = p2 // g3
    mesh_id = pl.DeviceIdType.MESH

    def rows_of(ref, start, size):
        return ref.at[pl.ds(pl.multiple_of(start, size), size), :]

    def exchange(stage, g, stride, mine, src_of, dst_of):
        def copy(s):
            j = lax.rem(mine + s, g)
            return pltpu.make_async_remote_copy(
                src_ref=src_of(j),
                dst_ref=dst_of(j, s),
                send_sem=send_sems.at[stage, s],
                recv_sem=recv_sems.at[stage, s],
                device_id=(me + (j - mine) * stride, col),
                device_id_type=mesh_id,
            )

        @pl.loop(1, g)
        def _(s):
            copy(s).start()

        @pl.loop(1, g)
        def _(s):
            copy(s).wait()

    def reduce_stage(stage, g, stride, mine, src, piece, recv):
        exchange(stage, g, stride, mine, lambda j: rows_of(src, j * piece, piece), lambda j, s: recv.at[s])
        return lax.fori_loop(1, g, lambda s, acc: acc + recv[s], src[pl.ds(pl.multiple_of(mine * piece, piece), piece), :])

    buf1[...] = reduce_stage(0, g1, s1, i1, x_ref, p1, recv1)
    buf2[...] = reduce_stage(1, g2, s2, i2, buf1, p2, recv2)
    base3 = i1 * p1 + i2 * p2
    reduced = reduce_stage(2, g3, s3, i3, buf2, p3, recv3)
    o_ref[pl.ds(pl.multiple_of(base3 + i3 * p3, p3), p3), :] = lax.dot_general(
        reduced, t_ref[...], (((1,), (1,)), ((), ())), precision=lax.Precision.HIGHEST, preferred_element_type=jnp.float32
    )

    def gather_stage(stage, g, stride, mine, base, block):
        own = rows_of(o_ref, base + mine * block, block)
        exchange(stage, g, stride, mine, lambda j: own, lambda j, s: own)

    gather_stage(3, g3, s3, i3, base3, p3)
    gather_stage(4, g2, s2, i2, i1 * p1, p2)
    gather_stage(5, g1, s1, i1, 0, p1)


def row_allreduce_times(x, t, n):
    rows, cols = x.shape
    groups = (2, 4, n // 8)
    g1, g2, g3 = groups
    p1 = rows // g1
    p2 = p1 // g2
    p3 = p2 // g3
    return pl.pallas_call(
        functools.partial(_allreduce_kernel, groups),
        out_shape=jax.ShapeDtypeStruct((rows, cols), x.dtype),
        in_specs=[pl.BlockSpec(memory_space=pltpu.VMEM)] * 2,
        out_specs=pl.BlockSpec(memory_space=pltpu.VMEM),
        scratch_shapes=[
            pltpu.VMEM((p1, cols), x.dtype),
            pltpu.VMEM((p2, cols), x.dtype),
            pltpu.VMEM((g1, p1, cols), x.dtype),
            pltpu.VMEM((g2, p2, cols), x.dtype),
            pltpu.VMEM((g3, p3, cols), x.dtype),
            pltpu.SemaphoreType.DMA((6, max(groups))),
            pltpu.SemaphoreType.DMA((6, max(groups))),
        ],
        compiler_params=pltpu.CompilerParams(has_side_effects=True),
        cost_estimate=pl.CostEstimate(
            flops=rows * cols, transcendentals=0, bytes_accessed=4 * rows * cols * 4
        ),
    )(x, t)


def _col_gather_kernel(n, v_ref, o_ref, send_sems, recv_sems):
    me = lax.axis_index("col")
    row = lax.axis_index("row")
    w = v_ref.shape[1]
    own = o_ref.at[:, pl.ds(pl.multiple_of(me * w, w), w)]

    def copy(s):
        return pltpu.make_async_remote_copy(
            src_ref=v_ref,
            dst_ref=own,
            send_sem=send_sems.at[s],
            recv_sem=recv_sems.at[s],
            device_id=(row, lax.rem(me + s, n)),
            device_id_type=pl.DeviceIdType.MESH,
        )

    @pl.loop(1, n)
    def _(s):
        copy(s).start()

    own[...] = v_ref[...]

    @pl.loop(1, n)
    def _(s):
        copy(s).wait()


def col_gather(v, n):
    rows, w = v.shape
    return pl.pallas_call(
        functools.partial(_col_gather_kernel, n),
        out_shape=jax.ShapeDtypeStruct((rows, w * n), v.dtype),
        in_specs=[pl.BlockSpec(memory_space=pltpu.VMEM)],
        out_specs=pl.BlockSpec(memory_space=pltpu.VMEM),
        scratch_shapes=[pltpu.SemaphoreType.DMA((n,)), pltpu.SemaphoreType.DMA((n,))],
        compiler_params=pltpu.CompilerParams(has_side_effects=True),
        cost_estimate=pl.CostEstimate(flops=0, transcendentals=0, bytes_accessed=2 * rows * w * n * 4),
    )(v)


def on_device(n_row, n_col, eigen_vectors, panel_first, panel_second, factor_first, factor_second):
    vectors_second = col_gather(panel_second, n_col)
    vectors_second, panel_first = lax.optimization_barrier((vectors_second, panel_first))
    vectors_first = lax.all_gather(panel_first, "col", axis=1, tiled=True)
    updated = eigen_vectors
    for vectors, factor in ((vectors_second, factor_second), (vectors_first, factor_first)):
        partial_t = lax.dot_general(updated, vectors, (((0,), (0,)), ((), ())), precision=lax.Precision.HIGH, preferred_element_type=jnp.float32)
        applied_t = row_allreduce_times(partial_t, factor, n_row)
        updated = updated - lax.dot_general(vectors, applied_t, (((1,), (1,)), ((), ())), precision=lax.Precision.HIGH, preferred_element_type=jnp.float32)
    return updated


def solution(mesh):
    return jax.shard_map(
        functools.partial(on_device, mesh.shape["row"], mesh.shape["col"]),
        mesh=mesh,
        in_specs=(P("row", "col"), P("row", "col"), P("row", "col"), P(), P()),
        out_specs=P("row", "col"),
        check_vma=False,
    )
```

```python
import functools

import jax
import jax.numpy as jnp
from jax import lax
from jax.experimental import pallas as pl
from jax.experimental.pallas import tpu as pltpu
from jax.sharding import PartitionSpec as P


def local_dot(left, right):
    return jnp.dot(left, right, precision=lax.Precision.HIGHEST, preferred_element_type=jnp.float32)


def _allreduce_kernel(groups, x_ref, t_ref, o_ref, buf1, buf2, recv1, recv2, recv3, send_sems, recv_sems):
    me = lax.axis_index("row")
    col = lax.axis_index("col")
    g1, g2, g3 = groups
    s1, s2, s3 = 1, g1, g1 * g2
    i1 = lax.rem(me, g1)
    i2 = lax.rem(me // s2, g2)
    i3 = me // s3
    rows = x_ref.shape[0]
    p1 = rows // g1
    p2 = p1 // g2
    p3 = p2 // g3
    mesh_id = pl.DeviceIdType.MESH

    def rows_of(ref, start, size):
        return ref.at[pl.ds(pl.multiple_of(start, size), size), :]

    def exchange(stage, g, stride, mine, src_of, dst_of):
        def copy(s):
            j = lax.rem(mine + s, g)
            return pltpu.make_async_remote_copy(
                src_ref=src_of(j),
                dst_ref=dst_of(j, s),
                send_sem=send_sems.at[stage, s],
                recv_sem=recv_sems.at[stage, s],
                device_id=(me + (j - mine) * stride, col),
                device_id_type=mesh_id,
            )

        @pl.loop(1, g)
        def _(s):
            copy(s).start()

        @pl.loop(1, g)
        def _(s):
            copy(s).wait()

    def reduce_stage(stage, g, stride, mine, src, piece, recv):
        exchange(stage, g, stride, mine, lambda j: rows_of(src, j * piece, piece), lambda j, s: recv.at[s])
        return lax.fori_loop(1, g, lambda s, acc: acc + recv[s], src[pl.ds(pl.multiple_of(mine * piece, piece), piece), :])

    buf1[...] = reduce_stage(0, g1, s1, i1, x_ref, p1, recv1)
    buf2[...] = reduce_stage(1, g2, s2, i2, buf1, p2, recv2)
    base3 = i1 * p1 + i2 * p2
    reduced = reduce_stage(2, g3, s3, i3, buf2, p3, recv3)
    o_ref[pl.ds(pl.multiple_of(base3 + i3 * p3, p3), p3), :] = lax.dot_general(
        reduced, t_ref[...], (((1,), (1,)), ((), ())), precision=lax.Precision.HIGHEST, preferred_element_type=jnp.float32
    )

    def gather_stage(stage, g, stride, mine, base, block):
        own = rows_of(o_ref, base + mine * block, block)
        exchange(stage, g, stride, mine, lambda j: own, lambda j, s: own)

    gather_stage(3, g3, s3, i3, base3, p3)
    gather_stage(4, g2, s2, i2, i1 * p1, p2)
    gather_stage(5, g1, s1, i1, 0, p1)


def row_allreduce_times(x, t, n):
    rows, cols = x.shape
    groups = (2, min(4, n // 2), max(1, n // 8))
    g1, g2, g3 = groups
    p1 = rows // g1
    p2 = p1 // g2
    p3 = p2 // g3
    return pl.pallas_call(
        functools.partial(_allreduce_kernel, groups),
        out_shape=jax.ShapeDtypeStruct((rows, cols), x.dtype),
        in_specs=[pl.BlockSpec(memory_space=pltpu.VMEM)] * 2,
        out_specs=pl.BlockSpec(memory_space=pltpu.VMEM),
        scratch_shapes=[
            pltpu.VMEM((p1, cols), x.dtype),
            pltpu.VMEM((p2, cols), x.dtype),
            pltpu.VMEM((g1, p1, cols), x.dtype),
            pltpu.VMEM((g2, p2, cols), x.dtype),
            pltpu.VMEM((g3, p3, cols), x.dtype),
            pltpu.SemaphoreType.DMA((6, max(groups))),
            pltpu.SemaphoreType.DMA((6, max(groups))),
        ],
        compiler_params=pltpu.CompilerParams(has_side_effects=True),
        cost_estimate=pl.CostEstimate(
            flops=rows * cols, transcendentals=0, bytes_accessed=4 * rows * cols * 4
        ),
    )(x, t)


def _col_gather_kernel(n, v_ref, o_ref, send_sems, recv_sems):
    me = lax.axis_index("col")
    row = lax.axis_index("row")
    rows, w = v_ref.shape
    half = rows // 2
    left, right = lax.rem(me + n - 1, n), lax.rem(me + 1, n)

    def block(j):
        return o_ref.at[:, pl.ds(pl.multiple_of(j * w, w), w)]

    def send(src, dst, k, target):
        return pltpu.make_async_remote_copy(
            src_ref=src,
            dst_ref=dst,
            send_sem=send_sems.at[k],
            recv_sem=recv_sems.at[k],
            device_id=(row, target),
            device_id_type=pl.DeviceIdType.MESH,
        )

    to_right = send(v_ref, block(me), 0, right)
    to_left = send(v_ref, block(me), 1, left)
    to_right.start()
    to_left.start()
    block(me)[...] = v_ref[...]
    to_right.wait_recv()
    from_left = block(left)
    fwd_right = send(from_left.at[pl.ds(0, half), :], from_left.at[pl.ds(0, half), :], 2, right)
    fwd_right.start()
    to_left.wait_recv()
    from_right = block(right)
    fwd_left = send(from_right.at[pl.ds(half, half), :], from_right.at[pl.ds(half, half), :], 3, left)
    fwd_left.start()
    to_right.wait_send()
    to_left.wait_send()
    fwd_right.wait()
    fwd_left.wait()


def col_gather(v, n):
    assert n == 4
    rows, w = v.shape
    return pl.pallas_call(
        functools.partial(_col_gather_kernel, n),
        out_shape=jax.ShapeDtypeStruct((rows, w * n), v.dtype),
        in_specs=[pl.BlockSpec(memory_space=pltpu.VMEM)],
        out_specs=pl.BlockSpec(memory_space=pltpu.VMEM),
        scratch_shapes=[pltpu.SemaphoreType.DMA((n,)), pltpu.SemaphoreType.DMA((n,))],
        compiler_params=pltpu.CompilerParams(has_side_effects=True),
        cost_estimate=pl.CostEstimate(flops=0, transcendentals=0, bytes_accessed=2 * rows * w * n * 4),
    )(v)


def on_device(n_row, n_col, eigen_vectors, panel_first, panel_second, factor_first, factor_second):
    vectors_second = col_gather(panel_second, n_col)
    vectors_second, panel_first = lax.optimization_barrier((vectors_second, panel_first))
    vectors_first = lax.all_gather(panel_first, "col", axis=1, tiled=True)
    updated = eigen_vectors
    for vectors, factor in ((vectors_second, factor_second), (vectors_first, factor_first)):
        partial_t = lax.dot_general(updated, vectors, (((0,), (0,)), ((), ())), precision=lax.Precision.HIGH, preferred_element_type=jnp.float32)
        applied_t = row_allreduce_times(partial_t, factor, n_row)
        updated = updated - lax.dot_general(vectors, applied_t, (((1,), (1,)), ((), ())), precision=lax.Precision.HIGH, preferred_element_type=jnp.float32)
    return updated


def solution(mesh):
    return jax.shard_map(
        functools.partial(on_device, mesh.shape["row"], mesh.shape["col"]),
        mesh=mesh,
        in_specs=(P("row", "col"), P("row", "col"), P("row", "col"), P(), P()),
        out_specs=P("row", "col"),
        check_vma=False,
    )
```

```python
import functools

import jax
import jax.numpy as jnp
from jax import lax
from jax.experimental import pallas as pl
from jax.experimental.pallas import tpu as pltpu
from jax.sharding import PartitionSpec as P


def local_dot(left, right):
    return jnp.dot(left, right, precision=lax.Precision.HIGHEST, preferred_element_type=jnp.float32)


def _allreduce_kernel(groups, x_ref, t_ref, o_ref, buf1, buf2, recv1, recv2, recv3, send_sems, recv_sems):
    me = lax.axis_index("row")
    col = lax.axis_index("col")
    g1, g2, g3 = groups
    s1, s2, s3 = 1, g1, g1 * g2
    i1 = lax.rem(me, g1)
    i2 = lax.rem(me // s2, g2)
    i3 = me // s3
    rows = x_ref.shape[0]
    p1 = rows // g1
    p2 = p1 // g2
    p3 = p2 // g3
    mesh_id = pl.DeviceIdType.MESH

    def rows_of(ref, start, size):
        return ref.at[pl.ds(pl.multiple_of(start, size), size), :]

    def exchange(stage, g, stride, mine, src_of, dst_of):
        def copy(s):
            j = lax.rem(mine + s, g)
            return pltpu.make_async_remote_copy(
                src_ref=src_of(j),
                dst_ref=dst_of(j, s),
                send_sem=send_sems.at[stage, s],
                recv_sem=recv_sems.at[stage, s],
                device_id=(me + (j - mine) * stride, col),
                device_id_type=mesh_id,
            )

        @pl.loop(1, g)
        def _(s):
            copy(s).start()

        @pl.loop(1, g)
        def _(s):
            copy(s).wait()

    def reduce_stage(stage, g, stride, mine, src, piece, recv):
        exchange(stage, g, stride, mine, lambda j: rows_of(src, j * piece, piece), lambda j, s: recv.at[s])
        return lax.fori_loop(1, g, lambda s, acc: acc + recv[s], src[pl.ds(pl.multiple_of(mine * piece, piece), piece), :])

    buf1[...] = reduce_stage(0, g1, s1, i1, x_ref, p1, recv1)
    buf2[...] = reduce_stage(1, g2, s2, i2, buf1, p2, recv2)
    base3 = i1 * p1 + i2 * p2
    reduced = reduce_stage(2, g3, s3, i3, buf2, p3, recv3)
    o_ref[pl.ds(pl.multiple_of(base3 + i3 * p3, p3), p3), :] = lax.dot_general(
        reduced, t_ref[...], (((1,), (1,)), ((), ())), precision=lax.Precision.HIGHEST, preferred_element_type=jnp.float32
    )

    def gather_stage(stage, g, stride, mine, base, block):
        own = rows_of(o_ref, base + mine * block, block)
        exchange(stage, g, stride, mine, lambda j: own, lambda j, s: own)

    gather_stage(3, g3, s3, i3, base3, p3)
    gather_stage(4, g2, s2, i2, i1 * p1, p2)
    gather_stage(5, g1, s1, i1, 0, p1)


def row_allreduce_times(x, t, n):
    rows, cols = x.shape
    groups = (2, min(4, n // 2), max(1, n // 8))
    g1, g2, g3 = groups
    p1 = rows // g1
    p2 = p1 // g2
    p3 = p2 // g3
    return pl.pallas_call(
        functools.partial(_allreduce_kernel, groups),
        out_shape=jax.ShapeDtypeStruct((rows, cols), x.dtype),
        in_specs=[pl.BlockSpec(memory_space=pltpu.VMEM)] * 2,
        out_specs=pl.BlockSpec(memory_space=pltpu.VMEM),
        scratch_shapes=[
            pltpu.VMEM((p1, cols), x.dtype),
            pltpu.VMEM((p2, cols), x.dtype),
            pltpu.VMEM((g1, p1, cols), x.dtype),
            pltpu.VMEM((g2, p2, cols), x.dtype),
            pltpu.VMEM((g3, p3, cols), x.dtype),
            pltpu.SemaphoreType.DMA((6, max(groups))),
            pltpu.SemaphoreType.DMA((6, max(groups))),
        ],
        compiler_params=pltpu.CompilerParams(has_side_effects=True),
        cost_estimate=pl.CostEstimate(
            flops=rows * cols, transcendentals=0, bytes_accessed=4 * rows * cols * 4
        ),
    )(x, t)


def _col_gather_kernel(n, v_ref, o_ref, send_sems, recv_sems):
    me = lax.axis_index("col")
    row = lax.axis_index("row")
    rows, w = v_ref.shape
    half = rows // 2
    left, right = lax.rem(me + n - 1, n), lax.rem(me + 1, n)

    def block(j):
        return o_ref.at[:, pl.ds(pl.multiple_of(j * w, w), w)]

    def send(src, dst, k, target):
        return pltpu.make_async_remote_copy(
            src_ref=src,
            dst_ref=dst,
            send_sem=send_sems.at[k],
            recv_sem=recv_sems.at[k],
            device_id=(row, target),
            device_id_type=pl.DeviceIdType.MESH,
        )

    to_right = send(v_ref, block(me), 0, right)
    to_left = send(v_ref, block(me), 1, left)
    to_right.start()
    to_left.start()
    block(me)[...] = v_ref[...]
    to_right.wait_recv()
    from_left = block(left)
    fwd_right = send(from_left.at[pl.ds(0, half), :], from_left.at[pl.ds(0, half), :], 2, right)
    fwd_right.start()
    to_left.wait_recv()
    from_right = block(right)
    fwd_left = send(from_right.at[pl.ds(half, half), :], from_right.at[pl.ds(half, half), :], 3, left)
    fwd_left.start()
    to_right.wait_send()
    to_left.wait_send()
    fwd_right.wait()
    fwd_left.wait()


def col_gather(v, n):
    assert n == 4
    rows, w = v.shape
    return pl.pallas_call(
        functools.partial(_col_gather_kernel, n),
        out_shape=jax.ShapeDtypeStruct((rows, w * n), v.dtype),
        in_specs=[pl.BlockSpec(memory_space=pltpu.VMEM)],
        out_specs=pl.BlockSpec(memory_space=pltpu.VMEM),
        scratch_shapes=[pltpu.SemaphoreType.DMA((n,)), pltpu.SemaphoreType.DMA((n,))],
        compiler_params=pltpu.CompilerParams(has_side_effects=True),
        cost_estimate=pl.CostEstimate(flops=0, transcendentals=0, bytes_accessed=2 * rows * w * n * 4),
    )(v)


def on_device(n_row, n_col, eigen_vectors, panel_first, panel_second, factor_first, factor_second):
    half = panel_second.shape[0] // 2
    upper = lax.all_gather(panel_second[:half], "col", axis=1, tiled=True)
    lower = col_gather(panel_second[half:], n_col)
    vectors_second = jnp.concatenate([upper, lower], axis=0)
    vectors_second, panel_first = lax.optimization_barrier((vectors_second, panel_first))
    vectors_first = lax.all_gather(panel_first, "col", axis=1, tiled=True)
    updated = eigen_vectors
    for vectors, factor in ((vectors_second, factor_second), (vectors_first, factor_first)):
        partial_t = lax.dot_general(updated, vectors, (((0,), (0,)), ((), ())), precision=lax.Precision.HIGH, preferred_element_type=jnp.float32)
        applied_t = row_allreduce_times(partial_t, factor, n_row)
        updated = updated - lax.dot_general(vectors, applied_t, (((1,), (1,)), ((), ())), precision=lax.Precision.HIGH, preferred_element_type=jnp.float32)
    return updated


def solution(mesh):
    return jax.shard_map(
        functools.partial(on_device, mesh.shape["row"], mesh.shape["col"]),
        mesh=mesh,
        in_specs=(P("row", "col"), P("row", "col"), P("row", "col"), P(), P()),
        out_specs=P("row", "col"),
        check_vma=False,
    )
```

```python
import functools

import jax
import jax.numpy as jnp
from jax import lax
from jax.experimental import pallas as pl
from jax.experimental.pallas import tpu as pltpu
from jax.sharding import PartitionSpec as P


def local_dot(left, right):
    return jnp.dot(left, right, precision=lax.Precision.HIGHEST, preferred_element_type=jnp.float32)


def _allreduce_kernel(groups, x_ref, t_ref, o_ref, buf1, buf2, recv1, recv2, recv3, send_sems, recv_sems):
    me = lax.axis_index("row")
    col = lax.axis_index("col")
    g1, g2, g3 = groups
    s1, s2, s3 = 1, g1, g1 * g2
    i1 = lax.rem(me, g1)
    i2 = lax.rem(me // s2, g2)
    i3 = me // s3
    rows = x_ref.shape[0]
    p1 = rows // g1
    p2 = p1 // g2
    p3 = p2 // g3
    mesh_id = pl.DeviceIdType.MESH

    def rows_of(ref, start, size):
        return ref.at[pl.ds(pl.multiple_of(start, size), size), :]

    barrier = pltpu.get_barrier_semaphore()
    for g, stride, mine in ((g1, s1, i1), (g2, s2, i2), (g3, s3, i3)):

        @pl.loop(1, g)
        def _(s):
            j = lax.rem(mine + s, g)
            pl.semaphore_signal(barrier, inc=1, device_id=(me + (j - mine) * stride, col), device_id_type=mesh_id)

    pl.semaphore_wait(barrier, g1 + g2 + g3 - 3)

    def exchange(stage, g, stride, mine, src_of, dst_of):
        def copy(s):
            j = lax.rem(mine + s, g)
            return pltpu.make_async_remote_copy(
                src_ref=src_of(j),
                dst_ref=dst_of(j, s),
                send_sem=send_sems.at[stage, s],
                recv_sem=recv_sems.at[stage, s],
                device_id=(me + (j - mine) * stride, col),
                device_id_type=mesh_id,
            )

        @pl.loop(1, g)
        def _(s):
            copy(s).start()

        @pl.loop(1, g)
        def _(s):
            copy(s).wait()

    def reduce_stage(stage, g, stride, mine, src, piece, recv):
        exchange(stage, g, stride, mine, lambda j: rows_of(src, j * piece, piece), lambda j, s: recv.at[s])
        return lax.fori_loop(1, g, lambda s, acc: acc + recv[s], src[pl.ds(pl.multiple_of(mine * piece, piece), piece), :])

    buf1[...] = reduce_stage(0, g1, s1, i1, x_ref, p1, recv1)
    buf2[...] = reduce_stage(1, g2, s2, i2, buf1, p2, recv2)
    base3 = i1 * p1 + i2 * p2
    reduced = reduce_stage(2, g3, s3, i3, buf2, p3, recv3)
    o_ref[pl.ds(pl.multiple_of(base3 + i3 * p3, p3), p3), :] = lax.dot_general(
        reduced, t_ref[...], (((1,), (1,)), ((), ())), precision=lax.Precision.HIGHEST, preferred_element_type=jnp.float32
    )

    def gather_stage(stage, g, stride, mine, base, block):
        own = rows_of(o_ref, base + mine * block, block)
        exchange(stage, g, stride, mine, lambda j: own, lambda j, s: own)

    gather_stage(3, g3, s3, i3, base3, p3)
    gather_stage(4, g2, s2, i2, i1 * p1, p2)
    gather_stage(5, g1, s1, i1, 0, p1)


def row_allreduce_times(x, t, n, collective_id):
    rows, cols = x.shape
    groups = (2, min(4, n // 2), max(1, n // 8))
    g1, g2, g3 = groups
    p1 = rows // g1
    p2 = p1 // g2
    p3 = p2 // g3
    return pl.pallas_call(
        functools.partial(_allreduce_kernel, groups),
        out_shape=jax.ShapeDtypeStruct((rows, cols), x.dtype),
        in_specs=[pl.BlockSpec(memory_space=pltpu.VMEM)] * 2,
        out_specs=pl.BlockSpec(memory_space=pltpu.VMEM),
        scratch_shapes=[
            pltpu.VMEM((p1, cols), x.dtype),
            pltpu.VMEM((p2, cols), x.dtype),
            pltpu.VMEM((g1, p1, cols), x.dtype),
            pltpu.VMEM((g2, p2, cols), x.dtype),
            pltpu.VMEM((g3, p3, cols), x.dtype),
            pltpu.SemaphoreType.DMA((6, max(groups))),
            pltpu.SemaphoreType.DMA((6, max(groups))),
        ],
        compiler_params=pltpu.CompilerParams(has_side_effects=True, collective_id=collective_id),
        cost_estimate=pl.CostEstimate(
            flops=rows * cols, transcendentals=0, bytes_accessed=4 * rows * cols * 4
        ),
    )(x, t)


def _col_gather_kernel(n, v_ref, o_ref, send_sems, recv_sems):
    me = lax.axis_index("col")
    row = lax.axis_index("row")
    rows, w = v_ref.shape
    half = rows // 2
    left, right = lax.rem(me + n - 1, n), lax.rem(me + 1, n)

    def block(j):
        return o_ref.at[:, pl.ds(pl.multiple_of(j * w, w), w)]

    def send(src, dst, k, target):
        return pltpu.make_async_remote_copy(
            src_ref=src,
            dst_ref=dst,
            send_sem=send_sems.at[k],
            recv_sem=recv_sems.at[k],
            device_id=(row, target),
            device_id_type=pl.DeviceIdType.MESH,
        )

    barrier = pltpu.get_barrier_semaphore()
    for target in (left, right):
        pl.semaphore_signal(barrier, inc=1, device_id=(row, target), device_id_type=pl.DeviceIdType.MESH)
    pl.semaphore_wait(barrier, 2)

    to_right = send(v_ref, block(me), 0, right)
    to_left = send(v_ref, block(me), 1, left)
    to_right.start()
    to_left.start()
    block(me)[...] = v_ref[...]
    to_right.wait_recv()
    from_left = block(left)
    fwd_right = send(from_left.at[pl.ds(0, half), :], from_left.at[pl.ds(0, half), :], 2, right)
    fwd_right.start()
    to_left.wait_recv()
    from_right = block(right)
    fwd_left = send(from_right.at[pl.ds(half, half), :], from_right.at[pl.ds(half, half), :], 3, left)
    fwd_left.start()
    to_right.wait_send()
    to_left.wait_send()
    fwd_right.wait()
    fwd_left.wait()


def col_gather(v, n):
    assert n == 4
    rows, w = v.shape
    return pl.pallas_call(
        functools.partial(_col_gather_kernel, n),
        out_shape=jax.ShapeDtypeStruct((rows, w * n), v.dtype),
        in_specs=[pl.BlockSpec(memory_space=pltpu.VMEM)],
        out_specs=pl.BlockSpec(memory_space=pltpu.VMEM),
        scratch_shapes=[pltpu.SemaphoreType.DMA((n,)), pltpu.SemaphoreType.DMA((n,))],
        compiler_params=pltpu.CompilerParams(has_side_effects=True, collective_id=0),
        cost_estimate=pl.CostEstimate(flops=0, transcendentals=0, bytes_accessed=2 * rows * w * n * 4),
    )(v)


def on_device(n_row, n_col, eigen_vectors, panel_first, panel_second, factor_first, factor_second):
    vectors_second = col_gather(panel_second, n_col)
    vectors_second, panel_first = lax.optimization_barrier((vectors_second, panel_first))
    vectors_first = lax.all_gather(panel_first, "col", axis=1, tiled=True)
    updated = eigen_vectors
    for collective_id, vectors, factor in ((1, vectors_second, factor_second), (2, vectors_first, factor_first)):
        partial_t = lax.dot_general(updated, vectors, (((0,), (0,)), ((), ())), precision=lax.Precision.HIGH, preferred_element_type=jnp.float32)
        applied_t = row_allreduce_times(partial_t, factor, n_row, collective_id)
        updated = updated - lax.dot_general(vectors, applied_t, (((1,), (1,)), ((), ())), precision=lax.Precision.HIGH, preferred_element_type=jnp.float32)
    return updated


def solution(mesh):
    return jax.shard_map(
        functools.partial(on_device, mesh.shape["row"], mesh.shape["col"]),
        mesh=mesh,
        in_specs=(P("row", "col"), P("row", "col"), P("row", "col"), P(), P()),
        out_specs=P("row", "col"),
        check_vma=False,
    )
```

```python
import functools

import jax
import jax.numpy as jnp
from jax import lax
from jax.experimental import pallas as pl
from jax.experimental.pallas import tpu as pltpu
from jax.sharding import PartitionSpec as P


def local_dot(left, right):
    return jnp.dot(left, right, precision=lax.Precision.HIGHEST, preferred_element_type=jnp.float32)


def _allreduce_kernel(groups, nc, x_ref, t_ref, o_ref, buf1, buf2, red, recv1, recv2, recv3, send_sems, recv_sems):
    me = lax.axis_index("row")
    col = lax.axis_index("col")
    g1, g2, g3 = groups
    s1, s2, s3 = 1, g1, g1 * g2
    i1 = lax.rem(me, g1)
    i2 = lax.rem(me // s2, g2)
    i3 = me // s3
    rows, cols = x_ref.shape
    cw = cols // nc
    p1 = rows // g1
    p2 = p1 // g2
    p3 = p2 // g3
    mesh_id = pl.DeviceIdType.MESH

    def part(ref, start, size, c):
        return ref.at[pl.ds(pl.multiple_of(start, size), size), pl.ds(c * cw, cw)]

    barrier = pltpu.get_barrier_semaphore()
    for g, stride, mine in ((g1, s1, i1), (g2, s2, i2), (g3, s3, i3)):

        @pl.loop(1, g)
        def _(s):
            j = lax.rem(mine + s, g)
            pl.semaphore_signal(barrier, inc=1, device_id=(me + (j - mine) * stride, col), device_id_type=mesh_id)

    pl.semaphore_wait(barrier, g1 + g2 + g3 - 3)

    def exchange(stage, c, g, stride, mine, src_of, dst_of):
        def copy(s):
            j = lax.rem(mine + s, g)
            return pltpu.make_async_remote_copy(
                src_ref=src_of(j),
                dst_ref=dst_of(j, s),
                send_sem=send_sems.at[stage, c, s],
                recv_sem=recv_sems.at[stage, c, s],
                device_id=(me + (j - mine) * stride, col),
                device_id_type=mesh_id,
            )

        def start():
            @pl.loop(1, g)
            def _(s):
                copy(s).start()

        def finish():
            @pl.loop(1, g)
            def _(s):
                copy(s).wait()

        return start, finish

    reduce_plan = (
        (0, g1, s1, i1, x_ref, p1, recv1, buf1),
        (1, g2, s2, i2, buf1, p2, recv2, buf2),
        (2, g3, s3, i3, buf2, p3, recv3, red),
    )

    def reduce_stage(stage, g, stride, mine, src, piece, recv, dst, c):
        start, finish = exchange(
            stage, c, g, stride, mine,
            lambda j: part(src, j * piece, piece, c),
            lambda j, s: recv.at[s, :, pl.ds(c * cw, cw)],
        )

        def combine():
            finish()
            own = src[pl.ds(pl.multiple_of(mine * piece, piece), piece), pl.ds(c * cw, cw)]
            dst[:, pl.ds(c * cw, cw)] = lax.fori_loop(1, g, lambda s, acc: acc + recv[s, :, pl.ds(c * cw, cw)], own)

        return start, combine

    def run(plan):
        for c in range(nc):
            plan[0](c)[0]()
        for k in range(len(plan)):
            for c in range(nc):
                plan[k](c)[1]()
                if k + 1 < len(plan):
                    plan[k + 1](c)[0]()

    run([functools.partial(reduce_stage, *p) for p in reduce_plan])

    base3 = i1 * p1 + i2 * p2
    o_ref[pl.ds(pl.multiple_of(base3 + i3 * p3, p3), p3), :] = lax.dot_general(
        red[...], t_ref[...], (((1,), (1,)), ((), ())), precision=lax.Precision.HIGHEST, preferred_element_type=jnp.float32
    )

    def gather_stage(stage, g, stride, mine, base, block, c):
        own = part(o_ref, base + mine * block, block, c)
        return exchange(stage, c, g, stride, mine, lambda j: own, lambda j, s: own)

    run([
        functools.partial(gather_stage, 3, g3, s3, i3, base3, p3),
        functools.partial(gather_stage, 4, g2, s2, i2, i1 * p1, p2),
        functools.partial(gather_stage, 5, g1, s1, i1, 0, p1),
    ])


def row_allreduce_times(x, t, n, collective_id, nc=2):
    rows, cols = x.shape
    groups = (2, min(4, n // 2), max(1, n // 8))
    g1, g2, g3 = groups
    p1 = rows // g1
    p2 = p1 // g2
    p3 = p2 // g3
    return pl.pallas_call(
        functools.partial(_allreduce_kernel, groups, nc),
        out_shape=jax.ShapeDtypeStruct((rows, cols), x.dtype),
        in_specs=[pl.BlockSpec(memory_space=pltpu.VMEM)] * 2,
        out_specs=pl.BlockSpec(memory_space=pltpu.VMEM),
        scratch_shapes=[
            pltpu.VMEM((p1, cols), x.dtype),
            pltpu.VMEM((p2, cols), x.dtype),
            pltpu.VMEM((p3, cols), x.dtype),
            pltpu.VMEM((g1, p1, cols), x.dtype),
            pltpu.VMEM((g2, p2, cols), x.dtype),
            pltpu.VMEM((g3, p3, cols), x.dtype),
            pltpu.SemaphoreType.DMA((6, nc, max(groups))),
            pltpu.SemaphoreType.DMA((6, nc, max(groups))),
        ],
        compiler_params=pltpu.CompilerParams(has_side_effects=True, collective_id=collective_id),
        cost_estimate=pl.CostEstimate(
            flops=rows * cols, transcendentals=0, bytes_accessed=4 * rows * cols * 4
        ),
    )(x, t)


def _col_gather_kernel(n, v_ref, o_ref, send_sems, recv_sems):
    me = lax.axis_index("col")
    row = lax.axis_index("row")
    rows, w = v_ref.shape
    half = rows // 2
    left, right = lax.rem(me + n - 1, n), lax.rem(me + 1, n)

    def block(j):
        return o_ref.at[:, pl.ds(pl.multiple_of(j * w, w), w)]

    def send(src, dst, k, target):
        return pltpu.make_async_remote_copy(
            src_ref=src,
            dst_ref=dst,
            send_sem=send_sems.at[k],
            recv_sem=recv_sems.at[k],
            device_id=(row, target),
            device_id_type=pl.DeviceIdType.MESH,
        )

    barrier = pltpu.get_barrier_semaphore()
    for target in (left, right):
        pl.semaphore_signal(barrier, inc=1, device_id=(row, target), device_id_type=pl.DeviceIdType.MESH)
    pl.semaphore_wait(barrier, 2)

    to_right = send(v_ref, block(me), 0, right)
    to_left = send(v_ref, block(me), 1, left)
    to_right.start()
    to_left.start()
    block(me)[...] = v_ref[...]
    to_right.wait_recv()
    from_left = block(left)
    fwd_right = send(from_left.at[pl.ds(0, half), :], from_left.at[pl.ds(0, half), :], 2, right)
    fwd_right.start()
    to_left.wait_recv()
    from_right = block(right)
    fwd_left = send(from_right.at[pl.ds(half, half), :], from_right.at[pl.ds(half, half), :], 3, left)
    fwd_left.start()
    to_right.wait_send()
    to_left.wait_send()
    fwd_right.wait()
    fwd_left.wait()


def col_gather(v, n):
    assert n == 4
    rows, w = v.shape
    return pl.pallas_call(
        functools.partial(_col_gather_kernel, n),
        out_shape=jax.ShapeDtypeStruct((rows, w * n), v.dtype),
        in_specs=[pl.BlockSpec(memory_space=pltpu.VMEM)],
        out_specs=pl.BlockSpec(memory_space=pltpu.VMEM),
        scratch_shapes=[pltpu.SemaphoreType.DMA((n,)), pltpu.SemaphoreType.DMA((n,))],
        compiler_params=pltpu.CompilerParams(has_side_effects=True, collective_id=0),
        cost_estimate=pl.CostEstimate(flops=0, transcendentals=0, bytes_accessed=2 * rows * w * n * 4),
    )(v)


def on_device(n_row, n_col, eigen_vectors, panel_first, panel_second, factor_first, factor_second):
    vectors_second = col_gather(panel_second, n_col)
    vectors_second, panel_first = lax.optimization_barrier((vectors_second, panel_first))
    vectors_first = lax.all_gather(panel_first, "col", axis=1, tiled=True)
    updated = eigen_vectors
    for collective_id, vectors, factor in ((1, vectors_second, factor_second), (2, vectors_first, factor_first)):
        partial_t = lax.dot_general(updated, vectors, (((0,), (0,)), ((), ())), precision=lax.Precision.HIGH, preferred_element_type=jnp.float32)
        applied_t = row_allreduce_times(partial_t, factor, n_row, collective_id)
        updated = updated - lax.dot_general(vectors, applied_t, (((1,), (1,)), ((), ())), precision=lax.Precision.HIGH, preferred_element_type=jnp.float32)
    return updated


def solution(mesh):
    return jax.shard_map(
        functools.partial(on_device, mesh.shape["row"], mesh.shape["col"]),
        mesh=mesh,
        in_specs=(P("row", "col"), P("row", "col"), P("row", "col"), P(), P()),
        out_specs=P("row", "col"),
        check_vma=False,
    )
```

```python
import functools

import jax
import jax.numpy as jnp
from jax import lax
from jax.experimental import pallas as pl
from jax.experimental.pallas import tpu as pltpu
from jax.sharding import PartitionSpec as P


def local_dot(left, right):
    return jnp.dot(left, right, precision=lax.Precision.HIGHEST, preferred_element_type=jnp.float32)


def _allreduce_kernel(groups, nc, x_ref, t_ref, o_ref, buf1, buf2, red, recv1, recv2, recv3, send_sems, recv_sems):
    me = lax.axis_index("row")
    col = lax.axis_index("col")
    g1, g2, g3 = groups
    s1, s2, s3 = 1, g1, g1 * g2
    i1 = lax.rem(me, g1)
    i2 = lax.rem(me // s2, g2)
    i3 = me // s3
    rows, cols = x_ref.shape
    cw = cols // nc
    p1 = rows // g1
    p2 = p1 // g2
    p3 = p2 // g3
    mesh_id = pl.DeviceIdType.MESH

    def part(ref, start, size, c):
        return ref.at[pl.ds(pl.multiple_of(start, size), size), pl.ds(c * cw, cw)]

    barrier = pltpu.get_barrier_semaphore()
    for g, stride, mine in ((g1, s1, i1), (g2, s2, i2), (g3, s3, i3)):

        @pl.loop(1, g)
        def _(s):
            j = lax.rem(mine + s, g)
            pl.semaphore_signal(barrier, inc=1, device_id=(me + (j - mine) * stride, col), device_id_type=mesh_id)

    pl.semaphore_wait(barrier, g1 + g2 + g3 - 3)

    def exchange(stage, c, g, stride, mine, src_of, dst_of):
        def copy(s):
            j = lax.rem(mine + s, g)
            return pltpu.make_async_remote_copy(
                src_ref=src_of(j),
                dst_ref=dst_of(j, s),
                send_sem=send_sems.at[stage, c, s],
                recv_sem=recv_sems.at[stage, c, s],
                device_id=(me + (j - mine) * stride, col),
                device_id_type=mesh_id,
            )

        def start():
            @pl.loop(1, g)
            def _(s):
                copy(s).start()

        def finish():
            @pl.loop(1, g)
            def _(s):
                copy(s).wait()

        return start, finish

    reduce_plan = (
        (0, g1, s1, i1, x_ref, p1, recv1, buf1),
        (1, g2, s2, i2, buf1, p2, recv2, buf2),
        (2, g3, s3, i3, buf2, p3, recv3, red),
    )

    def reduce_stage(stage, g, stride, mine, src, piece, recv, dst, c):
        start, finish = exchange(
            stage, c, g, stride, mine,
            lambda j: part(src, j * piece, piece, c),
            lambda j, s: recv.at[s, :, pl.ds(c * cw, cw)],
        )

        def combine():
            finish()
            own = src[pl.ds(pl.multiple_of(mine * piece, piece), piece), pl.ds(c * cw, cw)]
            dst[:, pl.ds(c * cw, cw)] = lax.fori_loop(1, g, lambda s, acc: acc + recv[s, :, pl.ds(c * cw, cw)], own)

        return start, combine

    def run(plan):
        for c in range(nc):
            plan[0](c)[0]()
        for k in range(len(plan)):
            for c in range(nc):
                plan[k](c)[1]()
                if k + 1 < len(plan):
                    plan[k + 1](c)[0]()

    run([functools.partial(reduce_stage, *p) for p in reduce_plan])

    base3 = i1 * p1 + i2 * p2
    o_ref[pl.ds(pl.multiple_of(base3 + i3 * p3, p3), p3), :] = lax.dot_general(
        red[...], t_ref[...], (((1,), (1,)), ((), ())), precision=lax.Precision.HIGHEST, preferred_element_type=jnp.float32
    )

    def gather_stage(stage, g, stride, mine, base, block, c):
        own = part(o_ref, base + mine * block, block, c)
        return exchange(stage, c, g, stride, mine, lambda j: own, lambda j, s: own)

    run([
        functools.partial(gather_stage, 3, g3, s3, i3, base3, p3),
        functools.partial(gather_stage, 4, g2, s2, i2, i1 * p1, p2),
        functools.partial(gather_stage, 5, g1, s1, i1, 0, p1),
    ])


def row_allreduce_times(x, t, n, collective_id, nc=2):
    rows, cols = x.shape
    groups = (2, min(4, n // 2), max(1, n // 8))
    g1, g2, g3 = groups
    p1 = rows // g1
    p2 = p1 // g2
    p3 = p2 // g3
    return pl.pallas_call(
        functools.partial(_allreduce_kernel, groups, nc),
        out_shape=jax.ShapeDtypeStruct((rows, cols), x.dtype),
        in_specs=[pl.BlockSpec(memory_space=pltpu.VMEM)] * 2,
        out_specs=pl.BlockSpec(memory_space=pltpu.VMEM),
        scratch_shapes=[
            pltpu.VMEM((p1, cols), x.dtype),
            pltpu.VMEM((p2, cols), x.dtype),
            pltpu.VMEM((p3, cols), x.dtype),
            pltpu.VMEM((g1, p1, cols), x.dtype),
            pltpu.VMEM((g2, p2, cols), x.dtype),
            pltpu.VMEM((g3, p3, cols), x.dtype),
            pltpu.SemaphoreType.DMA((6, nc, max(groups))),
            pltpu.SemaphoreType.DMA((6, nc, max(groups))),
        ],
        compiler_params=pltpu.CompilerParams(has_side_effects=True, collective_id=collective_id),
        cost_estimate=pl.CostEstimate(
            flops=rows * cols, transcendentals=0, bytes_accessed=4 * rows * cols * 4
        ),
    )(x, t)


def _col_gather_kernel(n, v_ref, o_ref, send_sems, recv_sems):
    me = lax.axis_index("col")
    row = lax.axis_index("row")
    rows, w = v_ref.shape
    half = rows // 2
    left, right = lax.rem(me + n - 1, n), lax.rem(me + 1, n)

    def block(j):
        return o_ref.at[:, pl.ds(pl.multiple_of(j * w, w), w)]

    def send(src, dst, k, target):
        return pltpu.make_async_remote_copy(
            src_ref=src,
            dst_ref=dst,
            send_sem=send_sems.at[k],
            recv_sem=recv_sems.at[k],
            device_id=(row, target),
            device_id_type=pl.DeviceIdType.MESH,
        )

    barrier = pltpu.get_barrier_semaphore()
    for target in (left, right):
        pl.semaphore_signal(barrier, inc=1, device_id=(row, target), device_id_type=pl.DeviceIdType.MESH)
    pl.semaphore_wait(barrier, 2)

    to_right = send(v_ref, block(me), 0, right)
    to_left = send(v_ref, block(me), 1, left)
    to_right.start()
    to_left.start()
    block(me)[...] = v_ref[...]
    to_right.wait_recv()
    from_left = block(left)
    fwd_right = send(from_left.at[pl.ds(0, half), :], from_left.at[pl.ds(0, half), :], 2, right)
    fwd_right.start()
    to_left.wait_recv()
    from_right = block(right)
    fwd_left = send(from_right.at[pl.ds(half, half), :], from_right.at[pl.ds(half, half), :], 3, left)
    fwd_left.start()
    to_right.wait_send()
    to_left.wait_send()
    fwd_right.wait()
    fwd_left.wait()


def col_gather(v, n):
    assert n == 4
    rows, w = v.shape
    return pl.pallas_call(
        functools.partial(_col_gather_kernel, n),
        out_shape=jax.ShapeDtypeStruct((rows, w * n), v.dtype),
        in_specs=[pl.BlockSpec(memory_space=pltpu.VMEM)],
        out_specs=pl.BlockSpec(memory_space=pltpu.VMEM),
        scratch_shapes=[pltpu.SemaphoreType.DMA((n,)), pltpu.SemaphoreType.DMA((n,))],
        compiler_params=pltpu.CompilerParams(has_side_effects=True, collective_id=0),
        cost_estimate=pl.CostEstimate(flops=0, transcendentals=0, bytes_accessed=2 * rows * w * n * 4),
    )(v)


def on_device(n_row, n_col, eigen_vectors, panel_first, panel_second, factor_first, factor_second):
    vectors_second = col_gather(panel_second, n_col)
    vectors_first = lax.all_gather(panel_first, "col", axis=1, tiled=True)
    updated = eigen_vectors
    for collective_id, vectors, factor in ((1, vectors_second, factor_second), (2, vectors_first, factor_first)):
        partial_t = lax.dot_general(updated, vectors, (((0,), (0,)), ((), ())), precision=lax.Precision.HIGH, preferred_element_type=jnp.float32)
        applied_t = row_allreduce_times(partial_t, factor, n_row, collective_id)
        updated = updated - lax.dot_general(vectors, applied_t, (((1,), (1,)), ((), ())), precision=lax.Precision.HIGH, preferred_element_type=jnp.float32)
    return updated


def solution(mesh):
    return jax.shard_map(
        functools.partial(on_device, mesh.shape["row"], mesh.shape["col"]),
        mesh=mesh,
        in_specs=(P("row", "col"), P("row", "col"), P("row", "col"), P(), P()),
        out_specs=P("row", "col"),
        check_vma=False,
    )
```

```python
import functools

import jax
import jax.numpy as jnp
from jax import lax
from jax.experimental import pallas as pl
from jax.experimental.pallas import tpu as pltpu
from jax.sharding import PartitionSpec as P


def local_dot(left, right):
    return jnp.dot(left, right, precision=lax.Precision.HIGHEST, preferred_element_type=jnp.float32)


def _allreduce_kernel(groups, nc, x_ref, t_ref, o_ref, buf1, buf2, red, relay, recv1, recv2, recv3, send_sems, recv_sems):
    me = lax.axis_index("row")
    col = lax.axis_index("col")
    g1, g2, g3 = groups
    s1, s2, s3 = 1, g1, g1 * g2
    i1 = lax.rem(me, g1)
    i2 = lax.rem(me // s2, g2)
    i3 = me // s3
    rows, cols = x_ref.shape
    cw = cols // nc
    p1 = rows // g1
    p2 = p1 // g2
    p3 = p2 // g3
    mesh_id = pl.DeviceIdType.MESH

    def part(ref, start, size, c):
        return ref.at[pl.ds(pl.multiple_of(start, size), size), pl.ds(c * cw, cw)]

    barrier = pltpu.get_barrier_semaphore()
    for g, stride, mine in ((g1, s1, i1), (g2, s2, i2), (g3, s3, i3)):

        @pl.loop(1, g)
        def _(s):
            j = lax.rem(mine + s, g)
            pl.semaphore_signal(barrier, inc=1, device_id=(me + (j - mine) * stride, col), device_id_type=mesh_id)

    pl.semaphore_wait(barrier, g1 + g2 + g3 - 3)

    def exchange(stage, c, g, stride, mine, src_of, dst_of):
        def copy(s):
            j = lax.rem(mine + s, g)
            return pltpu.make_async_remote_copy(
                src_ref=src_of(j),
                dst_ref=dst_of(j, s),
                send_sem=send_sems.at[stage, c, s],
                recv_sem=recv_sems.at[stage, c, s],
                device_id=(me + (j - mine) * stride, col),
                device_id_type=mesh_id,
            )

        def start():
            @pl.loop(1, g)
            def _(s):
                copy(s).start()

        def finish():
            @pl.loop(1, g)
            def _(s):
                copy(s).wait()

        return start, finish

    reduce_plan = (
        (0, g1, s1, i1, x_ref, p1, recv1, buf1),
        (1, g2, s2, i2, buf1, p2, recv2, buf2),
        (2, g3, s3, i3, buf2, p3, recv3, red),
    )

    def reduce_stage(stage, g, stride, mine, src, piece, recv, dst, c):
        start, finish = exchange(
            stage, c, g, stride, mine,
            lambda j: part(src, j * piece, piece, c),
            lambda j, s: recv.at[s, :, pl.ds(c * cw, cw)],
        )

        def combine():
            finish()
            own = src[pl.ds(pl.multiple_of(mine * piece, piece), piece), pl.ds(c * cw, cw)]
            dst[:, pl.ds(c * cw, cw)] = lax.fori_loop(1, g, lambda s, acc: acc + recv[s, :, pl.ds(c * cw, cw)], own)

        return start, combine

    def ring_reduce_stage(stage, g, stride, mine, src, piece, recv, dst, c):
        half = piece // 2
        right_i, left_i = lax.rem(mine + 1, g), lax.rem(mine + g - 1, g)
        right, left = me + (right_i - mine) * stride, me + (left_i - mine) * stride
        far = lax.rem(mine + 2, g)

        def send(src_ref, dst_ref, k, target):
            return pltpu.make_async_remote_copy(
                src_ref=src_ref, dst_ref=dst_ref,
                send_sem=send_sems.at[stage, c, k], recv_sem=recv_sems.at[stage, c, k],
                device_id=(target, col), device_id_type=mesh_id,
            )

        cols_c = pl.ds(c * cw, cw)
        first = [
            send(part(src, far * piece, half, c), recv.at[0, pl.ds(0, half), cols_c], 0, right),
            send(part(src, far * piece + half, half, c), recv.at[1, pl.ds(0, half), cols_c], 1, left),
        ]
        second = [
            send(relay.at[0, :, cols_c], recv.at[2, :, cols_c], 2, right),
            send(relay.at[1, :, cols_c], recv.at[3, :, cols_c], 3, left),
        ]

        def start():
            for cp in first:
                cp.start()

        def combine():
            for cp in first:
                cp.wait()
            for k, (j, lo) in enumerate(((right_i, 0), (left_i, half))):
                relay[k, :, cols_c] = src[pl.ds(pl.multiple_of(j * piece, piece), piece), cols_c]
                relay[k, pl.ds(lo, half), cols_c] += recv[k, pl.ds(0, half), cols_c]
            for cp in second:
                cp.start()
            for cp in second:
                cp.wait()
            own = src[pl.ds(pl.multiple_of(mine * piece, piece), piece), cols_c]
            dst[:, cols_c] = own + recv[2, :, cols_c] + recv[3, :, cols_c]

        return start, combine

    def run(plan):
        for c in range(nc):
            plan[0](c)[0]()
        for k in range(len(plan)):
            for c in range(nc):
                plan[k](c)[1]()
                if k + 1 < len(plan):
                    plan[k + 1](c)[0]()

    run([functools.partial(ring_reduce_stage if p[1] == 4 else reduce_stage, *p) for p in reduce_plan])

    base3 = i1 * p1 + i2 * p2
    o_ref[pl.ds(pl.multiple_of(base3 + i3 * p3, p3), p3), :] = lax.dot_general(
        red[...], t_ref[...], (((1,), (1,)), ((), ())), precision=lax.Precision.HIGHEST, preferred_element_type=jnp.float32
    )

    def gather_stage(stage, g, stride, mine, base, block, c):
        own = part(o_ref, base + mine * block, block, c)
        return exchange(stage, c, g, stride, mine, lambda j: own, lambda j, s: own)

    def ring_gather_stage(stage, g, stride, mine, base, block, c):
        half = block // 2
        right_i, left_i = lax.rem(mine + 1, g), lax.rem(mine + g - 1, g)
        right, left = me + (right_i - mine) * stride, me + (left_i - mine) * stride

        def send(view, k, target):
            return pltpu.make_async_remote_copy(
                src_ref=view, dst_ref=view,
                send_sem=send_sems.at[stage, c, k], recv_sem=recv_sems.at[stage, c, k],
                device_id=(target, col), device_id_type=mesh_id,
            )

        own = part(o_ref, base + mine * block, block, c)
        first = [send(own, 0, right), send(own, 1, left)]
        second = [
            send(part(o_ref, base + left_i * block, half, c), 2, right),
            send(part(o_ref, base + right_i * block + half, half, c), 3, left),
        ]

        def start():
            for cp in first:
                cp.start()

        def finish():
            first[0].wait_recv()
            second[0].start()
            first[1].wait_recv()
            second[1].start()
            for cp in first:
                cp.wait_send()
            for cp in second:
                cp.wait()

        return start, finish

    run([
        functools.partial(gather_stage, 3, g3, s3, i3, base3, p3),
        functools.partial(ring_gather_stage if g2 == 4 else gather_stage, 4, g2, s2, i2, i1 * p1, p2),
        functools.partial(gather_stage, 5, g1, s1, i1, 0, p1),
    ])


def row_allreduce_times(x, t, n, collective_id, nc=2):
    rows, cols = x.shape
    groups = (2, min(4, n // 2), max(1, n // 8))
    g1, g2, g3 = groups
    p1 = rows // g1
    p2 = p1 // g2
    p3 = p2 // g3
    return pl.pallas_call(
        functools.partial(_allreduce_kernel, groups, nc),
        out_shape=jax.ShapeDtypeStruct((rows, cols), x.dtype),
        in_specs=[pl.BlockSpec(memory_space=pltpu.VMEM)] * 2,
        out_specs=pl.BlockSpec(memory_space=pltpu.VMEM),
        scratch_shapes=[
            pltpu.VMEM((p1, cols), x.dtype),
            pltpu.VMEM((p2, cols), x.dtype),
            pltpu.VMEM((p3, cols), x.dtype),
            pltpu.VMEM((2, p2, cols), x.dtype),
            pltpu.VMEM((g1, p1, cols), x.dtype),
            pltpu.VMEM((g2, p2, cols), x.dtype),
            pltpu.VMEM((g3, p3, cols), x.dtype),
            pltpu.SemaphoreType.DMA((6, nc, max(groups))),
            pltpu.SemaphoreType.DMA((6, nc, max(groups))),
        ],
        compiler_params=pltpu.CompilerParams(has_side_effects=True, collective_id=collective_id),
        cost_estimate=pl.CostEstimate(
            flops=rows * cols, transcendentals=0, bytes_accessed=4 * rows * cols * 4
        ),
    )(x, t)


def _col_gather_kernel(n, v_ref, o_ref, send_sems, recv_sems):
    me = lax.axis_index("col")
    row = lax.axis_index("row")
    rows, w = v_ref.shape
    half = rows // 2
    left, right = lax.rem(me + n - 1, n), lax.rem(me + 1, n)

    def block(j):
        return o_ref.at[:, pl.ds(pl.multiple_of(j * w, w), w)]

    def send(src, dst, k, target):
        return pltpu.make_async_remote_copy(
            src_ref=src,
            dst_ref=dst,
            send_sem=send_sems.at[k],
            recv_sem=recv_sems.at[k],
            device_id=(row, target),
            device_id_type=pl.DeviceIdType.MESH,
        )

    barrier = pltpu.get_barrier_semaphore()
    for target in (left, right):
        pl.semaphore_signal(barrier, inc=1, device_id=(row, target), device_id_type=pl.DeviceIdType.MESH)
    pl.semaphore_wait(barrier, 2)

    to_right = send(v_ref, block(me), 0, right)
    to_left = send(v_ref, block(me), 1, left)
    to_right.start()
    to_left.start()
    block(me)[...] = v_ref[...]
    to_right.wait_recv()
    from_left = block(left)
    fwd_right = send(from_left.at[pl.ds(0, half), :], from_left.at[pl.ds(0, half), :], 2, right)
    fwd_right.start()
    to_left.wait_recv()
    from_right = block(right)
    fwd_left = send(from_right.at[pl.ds(half, half), :], from_right.at[pl.ds(half, half), :], 3, left)
    fwd_left.start()
    to_right.wait_send()
    to_left.wait_send()
    fwd_right.wait()
    fwd_left.wait()


def col_gather(v, n):
    assert n == 4
    rows, w = v.shape
    return pl.pallas_call(
        functools.partial(_col_gather_kernel, n),
        out_shape=jax.ShapeDtypeStruct((rows, w * n), v.dtype),
        in_specs=[pl.BlockSpec(memory_space=pltpu.VMEM)],
        out_specs=pl.BlockSpec(memory_space=pltpu.VMEM),
        scratch_shapes=[pltpu.SemaphoreType.DMA((n,)), pltpu.SemaphoreType.DMA((n,))],
        compiler_params=pltpu.CompilerParams(has_side_effects=True, collective_id=0),
        cost_estimate=pl.CostEstimate(flops=0, transcendentals=0, bytes_accessed=2 * rows * w * n * 4),
    )(v)


def on_device(n_row, n_col, eigen_vectors, panel_first, panel_second, factor_first, factor_second):
    vectors_second = col_gather(panel_second, n_col)
    vectors_second, panel_first = lax.optimization_barrier((vectors_second, panel_first))
    vectors_first = lax.all_gather(panel_first, "col", axis=1, tiled=True)
    updated = eigen_vectors
    for collective_id, vectors, factor in ((1, vectors_second, factor_second), (2, vectors_first, factor_first)):
        partial_t = lax.dot_general(updated, vectors, (((0,), (0,)), ((), ())), precision=lax.Precision.HIGH, preferred_element_type=jnp.float32)
        applied_t = row_allreduce_times(partial_t, factor, n_row, collective_id)
        updated = updated - lax.dot_general(vectors, applied_t, (((1,), (1,)), ((), ())), precision=lax.Precision.HIGH, preferred_element_type=jnp.float32)
    return updated


def solution(mesh):
    return jax.shard_map(
        functools.partial(on_device, mesh.shape["row"], mesh.shape["col"]),
        mesh=mesh,
        in_specs=(P("row", "col"), P("row", "col"), P("row", "col"), P(), P()),
        out_specs=P("row", "col"),
        check_vma=False,
    )
```

```python
import functools

import jax
import jax.numpy as jnp
from jax import lax
from jax.experimental import pallas as pl
from jax.experimental.pallas import tpu as pltpu
from jax.sharding import PartitionSpec as P


def local_dot(left, right):
    return jnp.dot(left, right, precision=lax.Precision.HIGHEST, preferred_element_type=jnp.float32)


def _allreduce_kernel(groups, nc, x_ref, t_ref, o_ref, buf1, buf2, red, recv1, recv2, recv3, send_sems, recv_sems):
    me = lax.axis_index("row")
    col = lax.axis_index("col")
    g1, g2, g3 = groups
    s1, s2, s3 = 1, g1, g1 * g2
    i1 = lax.rem(me, g1)
    i2 = lax.rem(me // s2, g2)
    i3 = me // s3
    rows, cols = x_ref.shape
    cw = cols // nc
    p1 = rows // g1
    p2 = p1 // g2
    p3 = p2 // g3
    mesh_id = pl.DeviceIdType.MESH

    def part(ref, start, size, c):
        return ref.at[pl.ds(pl.multiple_of(start, size), size), pl.ds(c * cw, cw)]

    barrier = pltpu.get_barrier_semaphore()
    for g, stride, mine in ((g1, s1, i1), (g2, s2, i2), (g3, s3, i3)):

        @pl.loop(1, g)
        def _(s):
            j = lax.rem(mine + s, g)
            pl.semaphore_signal(barrier, inc=1, device_id=(me + (j - mine) * stride, col), device_id_type=mesh_id)

    pl.semaphore_wait(barrier, g1 + g2 + g3 - 3)

    def exchange(stage, c, g, stride, mine, src_of, dst_of):
        def copy(s):
            j = lax.rem(mine + s, g)
            return pltpu.make_async_remote_copy(
                src_ref=src_of(j),
                dst_ref=dst_of(j, s),
                send_sem=send_sems.at[stage, c, s],
                recv_sem=recv_sems.at[stage, c, s],
                device_id=(me + (j - mine) * stride, col),
                device_id_type=mesh_id,
            )

        def start():
            @pl.loop(1, g)
            def _(s):
                copy(s).start()

        def finish():
            @pl.loop(1, g)
            def _(s):
                copy(s).wait()

        return start, finish

    reduce_plan = (
        (0, g1, s1, i1, x_ref, p1, recv1, buf1),
        (1, g2, s2, i2, buf1, p2, recv2, buf2),
        (2, g3, s3, i3, buf2, p3, recv3, red),
    )

    def reduce_stage(stage, g, stride, mine, src, piece, recv, dst, c):
        start, finish = exchange(
            stage, c, g, stride, mine,
            lambda j: part(src, j * piece, piece, c),
            lambda j, s: recv.at[s, :, pl.ds(c * cw, cw)],
        )

        def combine():
            finish()
            own = src[pl.ds(pl.multiple_of(mine * piece, piece), piece), pl.ds(c * cw, cw)]
            dst[:, pl.ds(c * cw, cw)] = lax.fori_loop(1, g, lambda s, acc: acc + recv[s, :, pl.ds(c * cw, cw)], own)

        return start, combine

    def run(plan):
        for c in range(nc):
            plan[0](c)[0]()
        for k in range(len(plan)):
            for c in range(nc):
                plan[k](c)[1]()
                if k + 1 < len(plan):
                    plan[k + 1](c)[0]()

    run([functools.partial(reduce_stage, *p) for p in reduce_plan])

    base3 = i1 * p1 + i2 * p2
    o_ref[pl.ds(pl.multiple_of(base3 + i3 * p3, p3), p3), :] = lax.dot_general(
        red[...], t_ref[...], (((1,), (1,)), ((), ())), precision=lax.Precision.HIGHEST, preferred_element_type=jnp.float32
    )

    def gather_stage(stage, g, stride, mine, base, block, c):
        own = part(o_ref, base + mine * block, block, c)
        return exchange(stage, c, g, stride, mine, lambda j: own, lambda j, s: own)

    run([
        functools.partial(gather_stage, 3, g3, s3, i3, base3, p3),
        functools.partial(gather_stage, 4, g2, s2, i2, i1 * p1, p2),
        functools.partial(gather_stage, 5, g1, s1, i1, 0, p1),
    ])


def row_allreduce_times(x, t, n, collective_id, nc=2):
    rows, cols = x.shape
    groups = (2, min(4, n // 2), max(1, n // 8))
    g1, g2, g3 = groups
    p1 = rows // g1
    p2 = p1 // g2
    p3 = p2 // g3
    return pl.pallas_call(
        functools.partial(_allreduce_kernel, groups, nc),
        out_shape=jax.ShapeDtypeStruct((rows, cols), x.dtype),
        in_specs=[pl.BlockSpec(memory_space=pltpu.VMEM)] * 2,
        out_specs=pl.BlockSpec(memory_space=pltpu.VMEM),
        scratch_shapes=[
            pltpu.VMEM((p1, cols), x.dtype),
            pltpu.VMEM((p2, cols), x.dtype),
            pltpu.VMEM((p3, cols), x.dtype),
            pltpu.VMEM((g1, p1, cols), x.dtype),
            pltpu.VMEM((g2, p2, cols), x.dtype),
            pltpu.VMEM((g3, p3, cols), x.dtype),
            pltpu.SemaphoreType.DMA((6, nc, max(groups))),
            pltpu.SemaphoreType.DMA((6, nc, max(groups))),
        ],
        compiler_params=pltpu.CompilerParams(has_side_effects=True, collective_id=collective_id),
        cost_estimate=pl.CostEstimate(
            flops=rows * cols, transcendentals=0, bytes_accessed=4 * rows * cols * 4
        ),
    )(x, t)


def _col_gather_kernel(n, v_ref, o_ref, send_sems, recv_sems):
    me = lax.axis_index("col")
    row = lax.axis_index("row")
    rows, w = v_ref.shape
    half = rows // 2
    left, right = lax.rem(me + n - 1, n), lax.rem(me + 1, n)

    def block(j):
        return o_ref.at[:, pl.ds(pl.multiple_of(j * w, w), w)]

    def send(src, dst, k, target):
        return pltpu.make_async_remote_copy(
            src_ref=src,
            dst_ref=dst,
            send_sem=send_sems.at[k],
            recv_sem=recv_sems.at[k],
            device_id=(row, target),
            device_id_type=pl.DeviceIdType.MESH,
        )

    barrier = pltpu.get_barrier_semaphore()
    for target in (left, right):
        pl.semaphore_signal(barrier, inc=1, device_id=(row, target), device_id_type=pl.DeviceIdType.MESH)
    pl.semaphore_wait(barrier, 2)

    def rows(view, lo):
        return view.at[pl.ds(lo, half), :]

    to_right = [send(rows(v_ref, lo), rows(block(me), lo), k, right) for k, lo in ((0, 0), (1, half))]
    to_left = [send(rows(v_ref, lo), rows(block(me), lo), k, left) for k, lo in ((2, half), (3, 0))]
    for a, b in zip(to_right, to_left):
        a.start()
        b.start()
    block(me)[...] = v_ref[...]
    to_right[0].wait_recv()
    fwd_right = send(rows(block(left), 0), rows(block(left), 0), 4, right)
    fwd_right.start()
    to_left[0].wait_recv()
    fwd_left = send(rows(block(right), half), rows(block(right), half), 5, left)
    fwd_left.start()
    for cp in to_right + to_left:
        cp.wait_send()
    to_right[1].wait_recv()
    to_left[1].wait_recv()
    fwd_right.wait()
    fwd_left.wait()


def col_gather(v, n):
    assert n == 4
    rows, w = v.shape
    return pl.pallas_call(
        functools.partial(_col_gather_kernel, n),
        out_shape=jax.ShapeDtypeStruct((rows, w * n), v.dtype),
        in_specs=[pl.BlockSpec(memory_space=pltpu.VMEM)],
        out_specs=pl.BlockSpec(memory_space=pltpu.VMEM),
        scratch_shapes=[pltpu.SemaphoreType.DMA((6,)), pltpu.SemaphoreType.DMA((6,))],
        compiler_params=pltpu.CompilerParams(has_side_effects=True, collective_id=0),
        cost_estimate=pl.CostEstimate(flops=0, transcendentals=0, bytes_accessed=2 * rows * w * n * 4),
    )(v)


def on_device(n_row, n_col, eigen_vectors, panel_first, panel_second, factor_first, factor_second):
    vectors_second = col_gather(panel_second, n_col)
    vectors_second, panel_first = lax.optimization_barrier((vectors_second, panel_first))
    vectors_first = lax.all_gather(panel_first, "col", axis=1, tiled=True)
    updated = eigen_vectors
    for collective_id, vectors, factor in ((1, vectors_second, factor_second), (2, vectors_first, factor_first)):
        partial_t = lax.dot_general(updated, vectors, (((0,), (0,)), ((), ())), precision=lax.Precision.HIGH, preferred_element_type=jnp.float32)
        applied_t = row_allreduce_times(partial_t, factor, n_row, collective_id)
        updated = updated - lax.dot_general(vectors, applied_t, (((1,), (1,)), ((), ())), precision=lax.Precision.HIGH, preferred_element_type=jnp.float32)
    return updated


def solution(mesh):
    return jax.shard_map(
        functools.partial(on_device, mesh.shape["row"], mesh.shape["col"]),
        mesh=mesh,
        in_specs=(P("row", "col"), P("row", "col"), P("row", "col"), P(), P()),
        out_specs=P("row", "col"),
        check_vma=False,
    )
```

```python
import functools

import jax
import jax.numpy as jnp
from jax import lax
from jax.experimental import pallas as pl
from jax.experimental.pallas import tpu as pltpu
from jax.sharding import PartitionSpec as P


def local_dot(left, right):
    return jnp.dot(left, right, precision=lax.Precision.HIGHEST, preferred_element_type=jnp.float32)


def _allreduce_kernel(groups, nc, x_ref, t_ref, o_ref, buf1, buf2, red, recv1, recv2, recv3, send_sems, recv_sems):
    me = lax.axis_index("row")
    col = lax.axis_index("col")
    g1, g2, g3 = groups
    s1, s2, s3 = 1, g1, g1 * g2
    i1 = lax.rem(me, g1)
    i2 = lax.rem(me // s2, g2)
    i3 = me // s3
    rows, cols = x_ref.shape
    cw = cols // nc
    p1 = rows // g1
    p2 = p1 // g2
    p3 = p2 // g3
    mesh_id = pl.DeviceIdType.MESH

    def part(ref, start, size, c):
        return ref.at[pl.ds(pl.multiple_of(start, size), size), pl.ds(c * cw, cw)]

    barrier = pltpu.get_barrier_semaphore()
    for g, stride, mine in ((g1, s1, i1), (g2, s2, i2), (g3, s3, i3)):

        @pl.loop(1, g)
        def _(s):
            j = lax.rem(mine + s, g)
            pl.semaphore_signal(barrier, inc=1, device_id=(me + (j - mine) * stride, col), device_id_type=mesh_id)

    pl.semaphore_wait(barrier, g1 + g2 + g3 - 3)

    def exchange(stage, c, g, stride, mine, src_of, dst_of):
        def copy(s):
            j = lax.rem(mine + s, g)
            return pltpu.make_async_remote_copy(
                src_ref=src_of(j),
                dst_ref=dst_of(j, s),
                send_sem=send_sems.at[stage, c, s],
                recv_sem=recv_sems.at[stage, c, s],
                device_id=(me + (j - mine) * stride, col),
                device_id_type=mesh_id,
            )

        def start():
            @pl.loop(1, g)
            def _(s):
                copy(s).start()

        def finish():
            @pl.loop(1, g)
            def _(s):
                copy(s).wait()

        return start, finish

    reduce_plan = (
        (0, g1, s1, i1, x_ref, p1, recv1, buf1),
        (1, g2, s2, i2, buf1, p2, recv2, buf2),
        (2, g3, s3, i3, buf2, p3, recv3, red),
    )

    def reduce_stage(stage, g, stride, mine, src, piece, recv, dst, c):
        start, finish = exchange(
            stage, c, g, stride, mine,
            lambda j: part(src, j * piece, piece, c),
            lambda j, s: recv.at[s, :, pl.ds(c * cw, cw)],
        )

        def combine():
            finish()
            own = src[pl.ds(pl.multiple_of(mine * piece, piece), piece), pl.ds(c * cw, cw)]
            dst[:, pl.ds(c * cw, cw)] = lax.fori_loop(1, g, lambda s, acc: acc + recv[s, :, pl.ds(c * cw, cw)], own)

        return start, combine

    def run(plan):
        for c in range(nc):
            plan[0](c)[0]()
        for k in range(len(plan)):
            for c in range(nc):
                plan[k](c)[1]()
                if k + 1 < len(plan):
                    plan[k + 1](c)[0]()

    run([functools.partial(reduce_stage, *p) for p in reduce_plan])

    base3 = i1 * p1 + i2 * p2
    o_ref[pl.ds(pl.multiple_of(base3 + i3 * p3, p3), p3), :] = lax.dot_general(
        red[...], t_ref[...], (((1,), (1,)), ((), ())), precision=lax.Precision.HIGHEST, preferred_element_type=jnp.float32
    )

    def gather_stage(stage, g, stride, mine, base, block, c):
        own = part(o_ref, base + mine * block, block, c)
        return exchange(stage, c, g, stride, mine, lambda j: own, lambda j, s: own)

    run([
        functools.partial(gather_stage, 3, g3, s3, i3, base3, p3),
        functools.partial(gather_stage, 4, g2, s2, i2, i1 * p1, p2),
        functools.partial(gather_stage, 5, g1, s1, i1, 0, p1),
    ])


def row_allreduce_times(x, t, n, collective_id, nc=4):
    rows, cols = x.shape
    groups = (2, min(4, n // 2), max(1, n // 8))
    g1, g2, g3 = groups
    p1 = rows // g1
    p2 = p1 // g2
    p3 = p2 // g3
    return pl.pallas_call(
        functools.partial(_allreduce_kernel, groups, nc),
        out_shape=jax.ShapeDtypeStruct((rows, cols), x.dtype),
        in_specs=[pl.BlockSpec(memory_space=pltpu.VMEM)] * 2,
        out_specs=pl.BlockSpec(memory_space=pltpu.VMEM),
        scratch_shapes=[
            pltpu.VMEM((p1, cols), x.dtype),
            pltpu.VMEM((p2, cols), x.dtype),
            pltpu.VMEM((p3, cols), x.dtype),
            pltpu.VMEM((g1, p1, cols), x.dtype),
            pltpu.VMEM((g2, p2, cols), x.dtype),
            pltpu.VMEM((g3, p3, cols), x.dtype),
            pltpu.SemaphoreType.DMA((6, nc, max(groups))),
            pltpu.SemaphoreType.DMA((6, nc, max(groups))),
        ],
        compiler_params=pltpu.CompilerParams(has_side_effects=True, collective_id=collective_id),
        cost_estimate=pl.CostEstimate(
            flops=rows * cols, transcendentals=0, bytes_accessed=4 * rows * cols * 4
        ),
    )(x, t)


def _col_gather_kernel(n, v_ref, o_ref, send_sems, recv_sems):
    me = lax.axis_index("col")
    row = lax.axis_index("row")
    rows, w = v_ref.shape
    half = rows // 2
    left, right = lax.rem(me + n - 1, n), lax.rem(me + 1, n)

    def block(j):
        return o_ref.at[:, pl.ds(pl.multiple_of(j * w, w), w)]

    def send(src, dst, k, target):
        return pltpu.make_async_remote_copy(
            src_ref=src,
            dst_ref=dst,
            send_sem=send_sems.at[k],
            recv_sem=recv_sems.at[k],
            device_id=(row, target),
            device_id_type=pl.DeviceIdType.MESH,
        )

    barrier = pltpu.get_barrier_semaphore()
    for target in (left, right):
        pl.semaphore_signal(barrier, inc=1, device_id=(row, target), device_id_type=pl.DeviceIdType.MESH)
    pl.semaphore_wait(barrier, 2)

    def rows(view, lo):
        return view.at[pl.ds(lo, half), :]

    to_right = [send(rows(v_ref, lo), rows(block(me), lo), k, right) for k, lo in ((0, 0), (1, half))]
    to_left = [send(rows(v_ref, lo), rows(block(me), lo), k, left) for k, lo in ((2, half), (3, 0))]
    for a, b in zip(to_right, to_left):
        a.start()
        b.start()
    block(me)[...] = v_ref[...]
    to_right[0].wait_recv()
    fwd_right = send(rows(block(left), 0), rows(block(left), 0), 4, right)
    fwd_right.start()
    to_left[0].wait_recv()
    fwd_left = send(rows(block(right), half), rows(block(right), half), 5, left)
    fwd_left.start()
    for cp in to_right + to_left:
        cp.wait_send()
    to_right[1].wait_recv()
    to_left[1].wait_recv()
    fwd_right.wait()
    fwd_left.wait()


def col_gather(v, n):
    assert n == 4
    rows, w = v.shape
    return pl.pallas_call(
        functools.partial(_col_gather_kernel, n),
        out_shape=jax.ShapeDtypeStruct((rows, w * n), v.dtype),
        in_specs=[pl.BlockSpec(memory_space=pltpu.VMEM)],
        out_specs=pl.BlockSpec(memory_space=pltpu.VMEM),
        scratch_shapes=[pltpu.SemaphoreType.DMA((6,)), pltpu.SemaphoreType.DMA((6,))],
        compiler_params=pltpu.CompilerParams(has_side_effects=True, collective_id=0),
        cost_estimate=pl.CostEstimate(flops=0, transcendentals=0, bytes_accessed=2 * rows * w * n * 4),
    )(v)


def on_device(n_row, n_col, eigen_vectors, panel_first, panel_second, factor_first, factor_second):
    vectors_second = col_gather(panel_second, n_col)
    vectors_second, panel_first = lax.optimization_barrier((vectors_second, panel_first))
    vectors_first = lax.all_gather(panel_first, "col", axis=1, tiled=True)
    updated = eigen_vectors
    for collective_id, vectors, factor in ((1, vectors_second, factor_second), (2, vectors_first, factor_first)):
        partial_t = lax.dot_general(updated, vectors, (((0,), (0,)), ((), ())), precision=lax.Precision.HIGH, preferred_element_type=jnp.float32)
        applied_t = row_allreduce_times(partial_t, factor, n_row, collective_id)
        updated = updated - lax.dot_general(vectors, applied_t, (((1,), (1,)), ((), ())), precision=lax.Precision.HIGH, preferred_element_type=jnp.float32)
    return updated


def solution(mesh):
    return jax.shard_map(
        functools.partial(on_device, mesh.shape["row"], mesh.shape["col"]),
        mesh=mesh,
        in_specs=(P("row", "col"), P("row", "col"), P("row", "col"), P(), P()),
        out_specs=P("row", "col"),
        check_vma=False,
    )
```

```python
import functools

import jax
import jax.numpy as jnp
from jax import lax
from jax.experimental import pallas as pl
from jax.experimental.pallas import tpu as pltpu
from jax.sharding import PartitionSpec as P


def local_dot(left, right):
    return jnp.dot(left, right, precision=lax.Precision.HIGHEST, preferred_element_type=jnp.float32)


def _allreduce_kernel(groups, nc, x_ref, t_ref, o_ref, buf1, buf2, red, recv1, recv2, recv3, send_sems, recv_sems):
    me = lax.axis_index("row")
    col = lax.axis_index("col")
    g1, g2, g3 = groups
    s1, s2, s3 = 1, g1, g1 * g2
    i1 = lax.rem(me, g1)
    i2 = lax.rem(me // s2, g2)
    i3 = me // s3
    rows, cols = x_ref.shape
    cw = cols // nc
    p1 = rows // g1
    p2 = p1 // g2
    p3 = p2 // g3
    mesh_id = pl.DeviceIdType.MESH

    def part(ref, start, size, c):
        return ref.at[pl.ds(pl.multiple_of(start, size), size), pl.ds(c * cw, cw)]

    barrier = pltpu.get_barrier_semaphore()
    for g, stride, mine in ((g1, s1, i1), (g2, s2, i2), (g3, s3, i3)):

        @pl.loop(1, g)
        def _(s):
            j = lax.rem(mine + s, g)
            pl.semaphore_signal(barrier, inc=1, device_id=(me + (j - mine) * stride, col), device_id_type=mesh_id)

    pl.semaphore_wait(barrier, g1 + g2 + g3 - 3)

    def exchange(stage, c, g, stride, mine, src_of, dst_of):
        def copy(s):
            j = lax.rem(mine + s, g)
            return pltpu.make_async_remote_copy(
                src_ref=src_of(j),
                dst_ref=dst_of(j, s),
                send_sem=send_sems.at[stage, c, s],
                recv_sem=recv_sems.at[stage, c, s],
                device_id=(me + (j - mine) * stride, col),
                device_id_type=mesh_id,
            )

        def start():
            @pl.loop(1, g)
            def _(s):
                copy(s).start()

        def finish():
            @pl.loop(1, g)
            def _(s):
                copy(s).wait()

        return start, finish

    reduce_plan = (
        (0, g1, s1, i1, x_ref, p1, recv1, buf1),
        (1, g2, s2, i2, buf1, p2, recv2, buf2),
        (2, g3, s3, i3, buf2, p3, recv3, red),
    )

    def reduce_stage(stage, g, stride, mine, src, piece, recv, dst, c):
        start, finish = exchange(
            stage, c, g, stride, mine,
            lambda j: part(src, j * piece, piece, c),
            lambda j, s: recv.at[s, :, pl.ds(c * cw, cw)],
        )

        def combine():
            finish()
            own = src[pl.ds(pl.multiple_of(mine * piece, piece), piece), pl.ds(c * cw, cw)]
            dst[:, pl.ds(c * cw, cw)] = lax.fori_loop(1, g, lambda s, acc: acc + recv[s, :, pl.ds(c * cw, cw)], own)

        return start, combine

    def run(plan):
        for c in range(nc):
            plan[0](c)[0]()
        for k in range(len(plan)):
            for c in range(nc):
                plan[k](c)[1]()
                if k + 1 < len(plan):
                    plan[k + 1](c)[0]()

    run([functools.partial(reduce_stage, *p) for p in reduce_plan])

    base3 = i1 * p1 + i2 * p2
    o_ref[pl.ds(pl.multiple_of(base3 + i3 * p3, p3), p3), :] = lax.dot_general(
        t_ref[...], red[...], (((1,), (1,)), ((), ())), precision=lax.Precision.HIGHEST, preferred_element_type=jnp.float32
    ).T

    def gather_stage(stage, g, stride, mine, base, block, c):
        own = part(o_ref, base + mine * block, block, c)
        return exchange(stage, c, g, stride, mine, lambda j: own, lambda j, s: own)

    run([
        functools.partial(gather_stage, 3, g3, s3, i3, base3, p3),
        functools.partial(gather_stage, 4, g2, s2, i2, i1 * p1, p2),
        functools.partial(gather_stage, 5, g1, s1, i1, 0, p1),
    ])


def row_allreduce_times(x, t, n, collective_id, nc=2):
    rows, cols = x.shape
    groups = (2, min(4, n // 2), max(1, n // 8))
    g1, g2, g3 = groups
    p1 = rows // g1
    p2 = p1 // g2
    p3 = p2 // g3
    return pl.pallas_call(
        functools.partial(_allreduce_kernel, groups, nc),
        out_shape=jax.ShapeDtypeStruct((rows, cols), x.dtype),
        in_specs=[pl.BlockSpec(memory_space=pltpu.VMEM)] * 2,
        out_specs=pl.BlockSpec(memory_space=pltpu.VMEM),
        scratch_shapes=[
            pltpu.VMEM((p1, cols), x.dtype),
            pltpu.VMEM((p2, cols), x.dtype),
            pltpu.VMEM((p3, cols), x.dtype),
            pltpu.VMEM((g1, p1, cols), x.dtype),
            pltpu.VMEM((g2, p2, cols), x.dtype),
            pltpu.VMEM((g3, p3, cols), x.dtype),
            pltpu.SemaphoreType.DMA((6, nc, max(groups))),
            pltpu.SemaphoreType.DMA((6, nc, max(groups))),
        ],
        compiler_params=pltpu.CompilerParams(has_side_effects=True, collective_id=collective_id),
        cost_estimate=pl.CostEstimate(
            flops=rows * cols, transcendentals=0, bytes_accessed=4 * rows * cols * 4
        ),
    )(x, t)


def _col_gather_kernel(n, v_ref, o_ref, send_sems, recv_sems):
    me = lax.axis_index("col")
    row = lax.axis_index("row")
    rows, w = v_ref.shape
    half = rows // 2
    left, right = lax.rem(me + n - 1, n), lax.rem(me + 1, n)

    def block(j):
        return o_ref.at[:, pl.ds(pl.multiple_of(j * w, w), w)]

    def send(src, dst, k, target):
        return pltpu.make_async_remote_copy(
            src_ref=src,
            dst_ref=dst,
            send_sem=send_sems.at[k],
            recv_sem=recv_sems.at[k],
            device_id=(row, target),
            device_id_type=pl.DeviceIdType.MESH,
        )

    barrier = pltpu.get_barrier_semaphore()
    for target in (left, right):
        pl.semaphore_signal(barrier, inc=1, device_id=(row, target), device_id_type=pl.DeviceIdType.MESH)
    pl.semaphore_wait(barrier, 2)

    def rows(view, lo):
        return view.at[pl.ds(lo, half), :]

    to_right = [send(rows(v_ref, lo), rows(block(me), lo), k, right) for k, lo in ((0, 0), (1, half))]
    to_left = [send(rows(v_ref, lo), rows(block(me), lo), k, left) for k, lo in ((2, half), (3, 0))]
    for a, b in zip(to_right, to_left):
        a.start()
        b.start()
    block(me)[...] = v_ref[...]
    to_right[0].wait_recv()
    fwd_right = send(rows(block(left), 0), rows(block(left), 0), 4, right)
    fwd_right.start()
    to_left[0].wait_recv()
    fwd_left = send(rows(block(right), half), rows(block(right), half), 5, left)
    fwd_left.start()
    for cp in to_right + to_left:
        cp.wait_send()
    to_right[1].wait_recv()
    to_left[1].wait_recv()
    fwd_right.wait()
    fwd_left.wait()


def col_gather(v, n):
    assert n == 4
    rows, w = v.shape
    return pl.pallas_call(
        functools.partial(_col_gather_kernel, n),
        out_shape=jax.ShapeDtypeStruct((rows, w * n), v.dtype),
        in_specs=[pl.BlockSpec(memory_space=pltpu.VMEM)],
        out_specs=pl.BlockSpec(memory_space=pltpu.VMEM),
        scratch_shapes=[pltpu.SemaphoreType.DMA((6,)), pltpu.SemaphoreType.DMA((6,))],
        compiler_params=pltpu.CompilerParams(has_side_effects=True, collective_id=0),
        cost_estimate=pl.CostEstimate(flops=0, transcendentals=0, bytes_accessed=2 * rows * w * n * 4),
    )(v)


def on_device(n_row, n_col, eigen_vectors, panel_first, panel_second, factor_first, factor_second):
    vectors_second = col_gather(panel_second, n_col)
    vectors_second, panel_first = lax.optimization_barrier((vectors_second, panel_first))
    vectors_first = lax.all_gather(panel_first, "col", axis=1, tiled=True)
    updated = eigen_vectors
    for collective_id, vectors, factor in ((1, vectors_second, factor_second), (2, vectors_first, factor_first)):
        partial_t = lax.dot_general(updated, vectors, (((0,), (0,)), ((), ())), precision=lax.Precision.HIGH, preferred_element_type=jnp.float32)
        applied_t = row_allreduce_times(partial_t, factor, n_row, collective_id)
        updated = updated - lax.dot_general(vectors, applied_t, (((1,), (1,)), ((), ())), precision=lax.Precision.HIGH, preferred_element_type=jnp.float32)
    return updated


def solution(mesh):
    return jax.shard_map(
        functools.partial(on_device, mesh.shape["row"], mesh.shape["col"]),
        mesh=mesh,
        in_specs=(P("row", "col"), P("row", "col"), P("row", "col"), P(), P()),
        out_specs=P("row", "col"),
        check_vma=False,
    )
```

```python
import functools

import jax
import jax.numpy as jnp
from jax import lax
from jax.experimental import pallas as pl
from jax.experimental.pallas import tpu as pltpu
from jax.sharding import PartitionSpec as P


def local_dot(left, right):
    return jnp.dot(left, right, precision=lax.Precision.HIGHEST, preferred_element_type=jnp.float32)


def _allreduce_kernel(groups, nc, x_ref, t_ref, o_ref, buf1, buf2, red, recv1, recv2, recv3, send_sems, recv_sems):
    me = lax.axis_index("row")
    col = lax.axis_index("col")
    g1, g2, g3 = groups
    s1, s2, s3 = 1, g1, g1 * g2
    i1 = lax.rem(me, g1)
    i2 = lax.rem(me // s2, g2)
    i3 = me // s3
    rows, cols = x_ref.shape
    cw = cols // nc
    p1 = rows // g1
    p2 = p1 // g2
    p3 = p2 // g3
    mesh_id = pl.DeviceIdType.MESH

    def part(ref, start, size, c):
        return ref.at[pl.ds(pl.multiple_of(start, size), size), cols_of(c)]

    def cols_of(c):
        return pl.ds(0, cols) if c is None else pl.ds(c * cw, cw)

    barrier = pltpu.get_barrier_semaphore()
    for g, stride, mine in ((g1, s1, i1), (g2, s2, i2), (g3, s3, i3)):

        @pl.loop(1, g)
        def _(s):
            j = lax.rem(mine + s, g)
            pl.semaphore_signal(barrier, inc=1, device_id=(me + (j - mine) * stride, col), device_id_type=mesh_id)

    pl.semaphore_wait(barrier, g1 + g2 + g3 - 3)

    def exchange(stage, c, g, stride, mine, src_of, dst_of):
        def copy(s):
            j = lax.rem(mine + s, g)
            return pltpu.make_async_remote_copy(
                src_ref=src_of(j),
                dst_ref=dst_of(j, s),
                send_sem=send_sems.at[stage, 0 if c is None else c, s],
                recv_sem=recv_sems.at[stage, 0 if c is None else c, s],
                device_id=(me + (j - mine) * stride, col),
                device_id_type=mesh_id,
            )

        def start():
            @pl.loop(1, g)
            def _(s):
                copy(s).start()

        def finish():
            @pl.loop(1, g)
            def _(s):
                copy(s).wait()

        return start, finish

    reduce_plan = (
        (0, g1, s1, i1, x_ref, p1, recv1, buf1),
        (1, g2, s2, i2, buf1, p2, recv2, buf2),
        (2, g3, s3, i3, buf2, p3, recv3, red),
    )

    def reduce_stage(stage, g, stride, mine, src, piece, recv, dst, c):
        start, finish = exchange(
            stage, c, g, stride, mine,
            lambda j: part(src, j * piece, piece, c),
            lambda j, s: recv.at[s, :, cols_of(c)],
        )

        def combine():
            finish()
            own = src[pl.ds(pl.multiple_of(mine * piece, piece), piece), cols_of(c)]
            dst[:, cols_of(c)] = lax.fori_loop(1, g, lambda s, acc: acc + recv[s, :, cols_of(c)], own)

        return start, combine

    def run(plan, whole):
        chunks = [[None] if k in whole else list(range(nc)) for k in range(len(plan))]
        for c in chunks[0]:
            plan[0](c)[0]()
        for k in range(len(plan)):
            if k + 1 < len(plan) and chunks[k + 1] != chunks[k]:
                for c in chunks[k]:
                    plan[k](c)[1]()
                for c in chunks[k + 1]:
                    plan[k + 1](c)[0]()
                continue
            for c in chunks[k]:
                plan[k](c)[1]()
                if k + 1 < len(plan):
                    plan[k + 1](c)[0]()

    run([functools.partial(reduce_stage, *p) for p in reduce_plan], whole=(2,))

    base3 = i1 * p1 + i2 * p2
    o_ref[pl.ds(pl.multiple_of(base3 + i3 * p3, p3), p3), :] = lax.dot_general(
        t_ref[...], red[...], (((1,), (1,)), ((), ())), precision=lax.Precision.HIGHEST, preferred_element_type=jnp.float32
    ).T

    def gather_stage(stage, g, stride, mine, base, block, c):
        own = part(o_ref, base + mine * block, block, c)
        return exchange(stage, c, g, stride, mine, lambda j: own, lambda j, s: own)

    run([
        functools.partial(gather_stage, 3, g3, s3, i3, base3, p3),
        functools.partial(gather_stage, 4, g2, s2, i2, i1 * p1, p2),
        functools.partial(gather_stage, 5, g1, s1, i1, 0, p1),
    ], whole=(0,))


def row_allreduce_times(x, t, n, collective_id, nc=2):
    rows, cols = x.shape
    groups = (2, min(4, n // 2), max(1, n // 8))
    g1, g2, g3 = groups
    p1 = rows // g1
    p2 = p1 // g2
    p3 = p2 // g3
    return pl.pallas_call(
        functools.partial(_allreduce_kernel, groups, nc),
        out_shape=jax.ShapeDtypeStruct((rows, cols), x.dtype),
        in_specs=[pl.BlockSpec(memory_space=pltpu.VMEM)] * 2,
        out_specs=pl.BlockSpec(memory_space=pltpu.VMEM),
        scratch_shapes=[
            pltpu.VMEM((p1, cols), x.dtype),
            pltpu.VMEM((p2, cols), x.dtype),
            pltpu.VMEM((p3, cols), x.dtype),
            pltpu.VMEM((g1, p1, cols), x.dtype),
            pltpu.VMEM((g2, p2, cols), x.dtype),
            pltpu.VMEM((g3, p3, cols), x.dtype),
            pltpu.SemaphoreType.DMA((6, nc, max(groups))),
            pltpu.SemaphoreType.DMA((6, nc, max(groups))),
        ],
        compiler_params=pltpu.CompilerParams(has_side_effects=True, collective_id=collective_id),
        cost_estimate=pl.CostEstimate(
            flops=rows * cols, transcendentals=0, bytes_accessed=4 * rows * cols * 4
        ),
    )(x, t)


def _col_gather_kernel(n, v_ref, o_ref, send_sems, recv_sems):
    me = lax.axis_index("col")
    row = lax.axis_index("row")
    rows, w = v_ref.shape
    half = rows // 2
    left, right = lax.rem(me + n - 1, n), lax.rem(me + 1, n)

    def block(j):
        return o_ref.at[:, pl.ds(pl.multiple_of(j * w, w), w)]

    def send(src, dst, k, target):
        return pltpu.make_async_remote_copy(
            src_ref=src,
            dst_ref=dst,
            send_sem=send_sems.at[k],
            recv_sem=recv_sems.at[k],
            device_id=(row, target),
            device_id_type=pl.DeviceIdType.MESH,
        )

    barrier = pltpu.get_barrier_semaphore()
    for target in (left, right):
        pl.semaphore_signal(barrier, inc=1, device_id=(row, target), device_id_type=pl.DeviceIdType.MESH)
    pl.semaphore_wait(barrier, 2)

    def rows(view, lo):
        return view.at[pl.ds(lo, half), :]

    to_right = [send(rows(v_ref, lo), rows(block(me), lo), k, right) for k, lo in ((0, 0), (1, half))]
    to_left = [send(rows(v_ref, lo), rows(block(me), lo), k, left) for k, lo in ((2, half), (3, 0))]
    for a, b in zip(to_right, to_left):
        a.start()
        b.start()
    block(me)[...] = v_ref[...]
    to_right[0].wait_recv()
    fwd_right = send(rows(block(left), 0), rows(block(left), 0), 4, right)
    fwd_right.start()
    to_left[0].wait_recv()
    fwd_left = send(rows(block(right), half), rows(block(right), half), 5, left)
    fwd_left.start()
    for cp in to_right + to_left:
        cp.wait_send()
    to_right[1].wait_recv()
    to_left[1].wait_recv()
    fwd_right.wait()
    fwd_left.wait()


def col_gather(v, n):
    assert n == 4
    rows, w = v.shape
    return pl.pallas_call(
        functools.partial(_col_gather_kernel, n),
        out_shape=jax.ShapeDtypeStruct((rows, w * n), v.dtype),
        in_specs=[pl.BlockSpec(memory_space=pltpu.VMEM)],
        out_specs=pl.BlockSpec(memory_space=pltpu.VMEM),
        scratch_shapes=[pltpu.SemaphoreType.DMA((6,)), pltpu.SemaphoreType.DMA((6,))],
        compiler_params=pltpu.CompilerParams(has_side_effects=True, collective_id=0),
        cost_estimate=pl.CostEstimate(flops=0, transcendentals=0, bytes_accessed=2 * rows * w * n * 4),
    )(v)


def on_device(n_row, n_col, eigen_vectors, panel_first, panel_second, factor_first, factor_second):
    vectors_second = col_gather(panel_second, n_col)
    vectors_second, panel_first = lax.optimization_barrier((vectors_second, panel_first))
    vectors_first = lax.all_gather(panel_first, "col", axis=1, tiled=True)
    updated = eigen_vectors
    for collective_id, vectors, factor in ((1, vectors_second, factor_second), (2, vectors_first, factor_first)):
        partial_t = lax.dot_general(updated, vectors, (((0,), (0,)), ((), ())), precision=lax.Precision.HIGH, preferred_element_type=jnp.float32)
        applied_t = row_allreduce_times(partial_t, factor, n_row, collective_id)
        updated = updated - lax.dot_general(vectors, applied_t, (((1,), (1,)), ((), ())), precision=lax.Precision.HIGH, preferred_element_type=jnp.float32)
    return updated


def solution(mesh):
    return jax.shard_map(
        functools.partial(on_device, mesh.shape["row"], mesh.shape["col"]),
        mesh=mesh,
        in_specs=(P("row", "col"), P("row", "col"), P("row", "col"), P(), P()),
        out_specs=P("row", "col"),
        check_vma=False,
    )
```

```python
import functools

import jax
import jax.numpy as jnp
from jax import lax
from jax.experimental import pallas as pl
from jax.experimental.pallas import tpu as pltpu
from jax.sharding import PartitionSpec as P


def local_dot(left, right):
    return jnp.dot(left, right, precision=lax.Precision.HIGHEST, preferred_element_type=jnp.float32)


def _allreduce_kernel(groups, nc, x_ref, t_ref, o_ref, buf1, buf2, red, recv1, recv2, recv3, send_sems, recv_sems):
    me = lax.axis_index("row")
    col = lax.axis_index("col")
    g1, g2, g3 = groups
    s1, s2, s3 = 1, g1, g1 * g2
    i1 = lax.rem(me, g1)
    i2 = lax.rem(me // s2, g2)
    i3 = me // s3
    rows, cols = x_ref.shape
    cw = cols // nc
    p1 = rows // g1
    p2 = p1 // g2
    p3 = p2 // g3
    mesh_id = pl.DeviceIdType.MESH

    def part(ref, start, size, c):
        return ref.at[pl.ds(pl.multiple_of(start, size), size), pl.ds(c * cw, cw)]

    barrier = pltpu.get_barrier_semaphore()
    for g, stride, mine in ((g1, s1, i1), (g2, s2, i2), (g3, s3, i3)):

        @pl.loop(1, g)
        def _(s):
            j = lax.rem(mine + s, g)
            pl.semaphore_signal(barrier, inc=1, device_id=(me + (j - mine) * stride, col), device_id_type=mesh_id)

    pl.semaphore_wait(barrier, g1 + g2 + g3 - 3)

    def exchange(stage, c, g, stride, mine, src_of, dst_of):
        def copy(s):
            j = lax.rem(mine + s, g)
            return pltpu.make_async_remote_copy(
                src_ref=src_of(j),
                dst_ref=dst_of(j, s),
                send_sem=send_sems.at[stage, c, s],
                recv_sem=recv_sems.at[stage, c, s],
                device_id=(me + (j - mine) * stride, col),
                device_id_type=mesh_id,
            )

        def start():
            @pl.loop(1, g)
            def _(s):
                copy(s).start()

        def finish():
            @pl.loop(1, g)
            def _(s):
                copy(s).wait()

        return start, finish

    reduce_plan = (
        (0, g1, s1, i1, x_ref, p1, recv1, buf1),
        (1, g2, s2, i2, buf1, p2, recv2, buf2),
        (2, g3, s3, i3, buf2, p3, recv3, red),
    )

    def reduce_stage(stage, g, stride, mine, src, piece, recv, dst, c):
        start, finish = exchange(
            stage, c, g, stride, mine,
            lambda j: part(src, j * piece, piece, c),
            lambda j, s: recv.at[s, :, pl.ds(c * cw, cw)],
        )

        def combine():
            finish()
            own = src[pl.ds(pl.multiple_of(mine * piece, piece), piece), pl.ds(c * cw, cw)]
            dst[:, pl.ds(c * cw, cw)] = lax.fori_loop(1, g, lambda s, acc: acc + recv[s, :, pl.ds(c * cw, cw)], own)

        return start, combine

    def run(plan):
        for c in range(nc):
            plan[0](c)[0]()
        for k in range(len(plan)):
            for c in range(nc):
                plan[k](c)[1]()
                if k + 1 < len(plan):
                    plan[k + 1](c)[0]()

    run([functools.partial(reduce_stage, *p) for p in reduce_plan])

    base3 = i1 * p1 + i2 * p2
    o_ref[pl.ds(pl.multiple_of(base3 + i3 * p3, p3), p3), :] = lax.dot_general(
        t_ref[...], red[...], (((1,), (1,)), ((), ())), precision=lax.Precision.HIGHEST, preferred_element_type=jnp.float32
    ).T

    def gather_stage(stage, g, stride, mine, base, block, c):
        own = part(o_ref, base + mine * block, block, c)
        return exchange(stage, c, g, stride, mine, lambda j: own, lambda j, s: own)

    run([
        functools.partial(gather_stage, 3, g3, s3, i3, base3, p3),
        functools.partial(gather_stage, 4, g2, s2, i2, i1 * p1, p2),
        functools.partial(gather_stage, 5, g1, s1, i1, 0, p1),
    ])


def row_allreduce_times(x, t, n, collective_id, nc=2):
    rows, cols = x.shape
    groups = (2, min(4, n // 2), max(1, n // 8))
    g1, g2, g3 = groups
    p1 = rows // g1
    p2 = p1 // g2
    p3 = p2 // g3
    return pl.pallas_call(
        functools.partial(_allreduce_kernel, groups, nc),
        out_shape=jax.ShapeDtypeStruct((rows, cols), x.dtype),
        in_specs=[pl.BlockSpec(memory_space=pltpu.VMEM)] * 2,
        out_specs=pl.BlockSpec(memory_space=pltpu.VMEM),
        scratch_shapes=[
            pltpu.VMEM((p1, cols), x.dtype),
            pltpu.VMEM((p2, cols), x.dtype),
            pltpu.VMEM((p3, cols), x.dtype),
            pltpu.VMEM((g1, p1, cols), x.dtype),
            pltpu.VMEM((g2, p2, cols), x.dtype),
            pltpu.VMEM((g3, p3, cols), x.dtype),
            pltpu.SemaphoreType.DMA((6, nc, max(groups))),
            pltpu.SemaphoreType.DMA((6, nc, max(groups))),
        ],
        compiler_params=pltpu.CompilerParams(has_side_effects=True, collective_id=collective_id),
        cost_estimate=pl.CostEstimate(
            flops=rows * cols, transcendentals=0, bytes_accessed=4 * rows * cols * 4
        ),
    )(x, t)


def _col_gather_kernel(n, v_ref, e_ref, o_ref, s_ref, send_sems, recv_sems):
    me = lax.axis_index("col")
    row = lax.axis_index("row")
    rows, w = v_ref.shape
    half = rows // 2
    left, right = lax.rem(me + n - 1, n), lax.rem(me + 1, n)

    def block(j):
        return o_ref.at[:, pl.ds(pl.multiple_of(j * w, w), w)]

    def send(src, dst, k, target):
        return pltpu.make_async_remote_copy(
            src_ref=src,
            dst_ref=dst,
            send_sem=send_sems.at[k],
            recv_sem=recv_sems.at[k],
            device_id=(row, target),
            device_id_type=pl.DeviceIdType.MESH,
        )

    barrier = pltpu.get_barrier_semaphore()
    for target in (left, right):
        pl.semaphore_signal(barrier, inc=1, device_id=(row, target), device_id_type=pl.DeviceIdType.MESH)
    pl.semaphore_wait(barrier, 2)

    def rows(view, lo):
        return view.at[pl.ds(lo, half), :]

    to_right = [send(rows(v_ref, lo), rows(block(me), lo), k, right) for k, lo in ((0, 0), (1, half))]
    to_left = [send(rows(v_ref, lo), rows(block(me), lo), k, left) for k, lo in ((2, half), (3, 0))]
    for a, b in zip(to_right, to_left):
        a.start()
        b.start()
    block(me)[...] = v_ref[...]

    def project(j):
        s_ref[:, pl.ds(pl.multiple_of(j * w, w), w)] = lax.dot_general(
            e_ref[...], block(j)[...], (((0,), (0,)), ((), ())), precision=lax.Precision.HIGH, preferred_element_type=jnp.float32
        )

    project(me)
    to_right[0].wait_recv()
    fwd_right = send(rows(block(left), 0), rows(block(left), 0), 4, right)
    fwd_right.start()
    to_left[0].wait_recv()
    fwd_left = send(rows(block(right), half), rows(block(right), half), 5, left)
    fwd_left.start()
    for cp in to_right + to_left:
        cp.wait_send()
    to_right[1].wait_recv()
    project(left)
    to_left[1].wait_recv()
    project(right)
    fwd_right.wait()
    fwd_left.wait()
    project(lax.rem(me + 2, n))


def col_gather(v, e, n):
    assert n == 4
    rows, w = v.shape
    return pl.pallas_call(
        functools.partial(_col_gather_kernel, n),
        out_shape=(
            jax.ShapeDtypeStruct((rows, w * n), v.dtype),
            jax.ShapeDtypeStruct((e.shape[1], w * n), jnp.float32),
        ),
        in_specs=[pl.BlockSpec(memory_space=pltpu.VMEM)] * 2,
        out_specs=(pl.BlockSpec(memory_space=pltpu.VMEM), pl.BlockSpec(memory_space=pltpu.VMEM)),
        scratch_shapes=[pltpu.SemaphoreType.DMA((6,)), pltpu.SemaphoreType.DMA((6,))],
        compiler_params=pltpu.CompilerParams(has_side_effects=True, collective_id=0),
        cost_estimate=pl.CostEstimate(
            flops=2 * rows * e.shape[1] * w * n, transcendentals=0, bytes_accessed=2 * rows * w * n * 4 + rows * e.shape[1] * 4
        ),
    )(v, e)


def on_device(n_row, n_col, eigen_vectors, panel_first, panel_second, factor_first, factor_second):
    vectors_second, partial_second = col_gather(panel_second, eigen_vectors, n_col)
    vectors_second, panel_first = lax.optimization_barrier((vectors_second, panel_first))
    vectors_first = lax.all_gather(panel_first, "col", axis=1, tiled=True)
    updated = eigen_vectors
    for collective_id, vectors, factor in ((1, vectors_second, factor_second), (2, vectors_first, factor_first)):
        partial_t = partial_second if collective_id == 1 else lax.dot_general(updated, vectors, (((0,), (0,)), ((), ())), precision=lax.Precision.HIGH, preferred_element_type=jnp.float32)
        applied_t = row_allreduce_times(partial_t, factor, n_row, collective_id)
        updated = updated - lax.dot_general(vectors, applied_t, (((1,), (1,)), ((), ())), precision=lax.Precision.HIGH, preferred_element_type=jnp.float32)
    return updated


def solution(mesh):
    return jax.shard_map(
        functools.partial(on_device, mesh.shape["row"], mesh.shape["col"]),
        mesh=mesh,
        in_specs=(P("row", "col"), P("row", "col"), P("row", "col"), P(), P()),
        out_specs=P("row", "col"),
        check_vma=False,
    )
```

```python
import functools

import jax
import jax.numpy as jnp
from jax import lax
from jax.experimental import pallas as pl
from jax.experimental.pallas import tpu as pltpu
from jax.sharding import PartitionSpec as P


def local_dot(left, right):
    return jnp.dot(left, right, precision=lax.Precision.HIGHEST, preferred_element_type=jnp.float32)


def _allreduce_kernel(groups, nc, x_ref, t_ref, o_ref, buf1, buf2, red, recv1, recv2, recv3, send_sems, recv_sems):
    me = lax.axis_index("row")
    col = lax.axis_index("col")
    g1, g2, g3 = groups
    s1, s2, s3 = 1, g1, g1 * g2
    i1 = lax.rem(me, g1)
    i2 = lax.rem(me // s2, g2)
    i3 = me // s3
    rows, cols = x_ref.shape
    cw = cols // nc
    p1 = rows // g1
    p2 = p1 // g2
    p3 = p2 // g3
    mesh_id = pl.DeviceIdType.MESH

    def part(ref, start, size, c):
        return ref.at[pl.ds(pl.multiple_of(start, size), size), pl.ds(c * cw, cw)]

    barrier = pltpu.get_barrier_semaphore()
    for g, stride, mine in ((g1, s1, i1), (g2, s2, i2), (g3, s3, i3)):

        @pl.loop(1, g)
        def _(s):
            j = lax.rem(mine + s, g)
            pl.semaphore_signal(barrier, inc=1, device_id=(me + (j - mine) * stride, col), device_id_type=mesh_id)

    pl.semaphore_wait(barrier, g1 + g2 + g3 - 3)

    def exchange(stage, c, g, stride, mine, src_of, dst_of):
        def copy(s):
            j = lax.rem(mine + s, g)
            return pltpu.make_async_remote_copy(
                src_ref=src_of(j),
                dst_ref=dst_of(j, s),
                send_sem=send_sems.at[stage, c, s],
                recv_sem=recv_sems.at[stage, c, s],
                device_id=(me + (j - mine) * stride, col),
                device_id_type=mesh_id,
            )

        def start():
            @pl.loop(1, g)
            def _(s):
                copy(s).start()

        def finish():
            @pl.loop(1, g)
            def _(s):
                copy(s).wait()

        return start, finish

    reduce_plan = (
        (0, g1, s1, i1, x_ref, p1, recv1, buf1),
        (1, g2, s2, i2, buf1, p2, recv2, buf2),
        (2, g3, s3, i3, buf2, p3, recv3, red),
    )

    def reduce_stage(stage, g, stride, mine, src, piece, recv, dst, c):
        start, finish = exchange(
            stage, c, g, stride, mine,
            lambda j: part(src, j * piece, piece, c),
            lambda j, s: recv.at[s, :, pl.ds(c * cw, cw)],
        )

        def combine():
            finish()
            own = src[pl.ds(pl.multiple_of(mine * piece, piece), piece), pl.ds(c * cw, cw)]
            dst[:, pl.ds(c * cw, cw)] = lax.fori_loop(1, g, lambda s, acc: acc + recv[s, :, pl.ds(c * cw, cw)], own)

        return start, combine

    def run(plan):
        for c in range(nc):
            plan[0](c)[0]()
        for k in range(len(plan)):
            for c in range(nc):
                plan[k](c)[1]()
                if k + 1 < len(plan):
                    plan[k + 1](c)[0]()

    run([functools.partial(reduce_stage, *p) for p in reduce_plan])

    base3 = i1 * p1 + i2 * p2
    o_ref[pl.ds(pl.multiple_of(base3 + i3 * p3, p3), p3), :] = lax.dot_general(
        t_ref[...], red[...], (((1,), (1,)), ((), ())), precision=lax.Precision.HIGHEST, preferred_element_type=jnp.float32
    ).T

    def gather_stage(stage, g, stride, mine, base, block, c):
        own = part(o_ref, base + mine * block, block, c)
        return exchange(stage, c, g, stride, mine, lambda j: own, lambda j, s: own)

    run([
        functools.partial(gather_stage, 3, g3, s3, i3, base3, p3),
        functools.partial(gather_stage, 4, g2, s2, i2, i1 * p1, p2),
        functools.partial(gather_stage, 5, g1, s1, i1, 0, p1),
    ])


def row_allreduce_times(x, t, n, collective_id, nc=2):
    rows, cols = x.shape
    groups = (2, min(4, n // 2), max(1, n // 8))
    g1, g2, g3 = groups
    p1 = rows // g1
    p2 = p1 // g2
    p3 = p2 // g3
    return pl.pallas_call(
        functools.partial(_allreduce_kernel, groups, nc),
        out_shape=jax.ShapeDtypeStruct((rows, cols), x.dtype),
        in_specs=[pl.BlockSpec(memory_space=pltpu.VMEM)] * 2,
        out_specs=pl.BlockSpec(memory_space=pltpu.VMEM),
        scratch_shapes=[
            pltpu.VMEM((p1, cols), x.dtype),
            pltpu.VMEM((p2, cols), x.dtype),
            pltpu.VMEM((p3, cols), x.dtype),
            pltpu.VMEM((g1, p1, cols), x.dtype),
            pltpu.VMEM((g2, p2, cols), x.dtype),
            pltpu.VMEM((g3, p3, cols), x.dtype),
            pltpu.SemaphoreType.DMA((6, nc, max(groups))),
            pltpu.SemaphoreType.DMA((6, nc, max(groups))),
        ],
        compiler_params=pltpu.CompilerParams(has_side_effects=True, collective_id=collective_id),
        cost_estimate=pl.CostEstimate(
            flops=rows * cols, transcendentals=0, bytes_accessed=4 * rows * cols * 4
        ),
    )(x, t)


def _col_gather_kernel(n, v_ref, e_ref, o_ref, s_ref, send_sems, recv_sems):
    me = lax.axis_index("col")
    row = lax.axis_index("row")
    rows, w = v_ref.shape
    half = rows // 2
    left, right = lax.rem(me + n - 1, n), lax.rem(me + 1, n)

    def block(j):
        return o_ref.at[:, pl.ds(pl.multiple_of(j * w, w), w)]

    def send(src, dst, k, target):
        return pltpu.make_async_remote_copy(
            src_ref=src,
            dst_ref=dst,
            send_sem=send_sems.at[k],
            recv_sem=recv_sems.at[k],
            device_id=(row, target),
            device_id_type=pl.DeviceIdType.MESH,
        )

    barrier = pltpu.get_barrier_semaphore()
    for target in (left, right):
        pl.semaphore_signal(barrier, inc=1, device_id=(row, target), device_id_type=pl.DeviceIdType.MESH)
    pl.semaphore_wait(barrier, 2)

    def rows_of(view, lo):
        return view.at[pl.ds(lo, half), :]

    to_right = [send(rows_of(v_ref, lo), rows_of(block(me), lo), k, right) for k, lo in ((0, 0), (1, half))]
    to_left = [send(rows_of(v_ref, lo), rows_of(block(me), lo), k, left) for k, lo in ((2, half), (3, 0))]
    for a, b in zip(to_right, to_left):
        a.start()
        b.start()
    block(me)[...] = v_ref[...]

    def project(j, lo, size, add):
        cols = pl.ds(pl.multiple_of(j * w, w), w)
        part = lax.dot_general(
            e_ref[pl.ds(lo, size), :], block(j)[pl.ds(lo, size), :], (((0,), (0,)), ((), ())),
            precision=lax.Precision.HIGH, preferred_element_type=jnp.float32,
        )
        if add:
            s_ref[:, cols] += part
        else:
            s_ref[:, cols] = part

    project(me, 0, rows, False)
    to_right[0].wait_recv()
    fwd_right = send(rows_of(block(left), 0), rows_of(block(left), 0), 4, right)
    fwd_right.start()
    to_left[0].wait_recv()
    fwd_left = send(rows_of(block(right), half), rows_of(block(right), half), 5, left)
    fwd_left.start()
    project(left, 0, half, False)
    project(right, half, half, False)
    to_right[1].wait_recv()
    project(left, half, half, True)
    to_left[1].wait_recv()
    project(right, 0, half, True)
    far = lax.rem(me + 2, n)
    fwd_right.wait_recv()
    project(far, 0, half, False)
    fwd_left.wait_recv()
    project(far, half, half, True)
    for cp in to_right + to_left + [fwd_right, fwd_left]:
        cp.wait_send()


def col_gather(v, e, n):
    assert n == 4
    rows, w = v.shape
    return pl.pallas_call(
        functools.partial(_col_gather_kernel, n),
        out_shape=(
            jax.ShapeDtypeStruct((rows, w * n), v.dtype),
            jax.ShapeDtypeStruct((e.shape[1], w * n), jnp.float32),
        ),
        in_specs=[pl.BlockSpec(memory_space=pltpu.VMEM)] * 2,
        out_specs=(pl.BlockSpec(memory_space=pltpu.VMEM), pl.BlockSpec(memory_space=pltpu.VMEM)),
        scratch_shapes=[pltpu.SemaphoreType.DMA((6,)), pltpu.SemaphoreType.DMA((6,))],
        compiler_params=pltpu.CompilerParams(has_side_effects=True, collective_id=0),
        cost_estimate=pl.CostEstimate(
            flops=2 * rows * e.shape[1] * w * n, transcendentals=0, bytes_accessed=2 * rows * w * n * 4 + rows * e.shape[1] * 4
        ),
    )(v, e)


def on_device(n_row, n_col, eigen_vectors, panel_first, panel_second, factor_first, factor_second):
    vectors_second, partial_second = col_gather(panel_second, eigen_vectors, n_col)
    vectors_second, panel_first = lax.optimization_barrier((vectors_second, panel_first))
    vectors_first = lax.all_gather(panel_first, "col", axis=1, tiled=True)
    updated = eigen_vectors
    for collective_id, vectors, factor in ((1, vectors_second, factor_second), (2, vectors_first, factor_first)):
        partial_t = partial_second if collective_id == 1 else lax.dot_general(updated, vectors, (((0,), (0,)), ((), ())), precision=lax.Precision.HIGH, preferred_element_type=jnp.float32)
        applied_t = row_allreduce_times(partial_t, factor, n_row, collective_id)
        updated = updated - lax.dot_general(vectors, applied_t, (((1,), (1,)), ((), ())), precision=lax.Precision.HIGH, preferred_element_type=jnp.float32)
    return updated


def solution(mesh):
    return jax.shard_map(
        functools.partial(on_device, mesh.shape["row"], mesh.shape["col"]),
        mesh=mesh,
        in_specs=(P("row", "col"), P("row", "col"), P("row", "col"), P(), P()),
        out_specs=P("row", "col"),
        check_vma=False,
    )
```

```python
import functools

import jax
import jax.numpy as jnp
from jax import lax
from jax.experimental import pallas as pl
from jax.experimental.pallas import tpu as pltpu
from jax.sharding import PartitionSpec as P


def local_dot(left, right):
    return jnp.dot(left, right, precision=lax.Precision.HIGHEST, preferred_element_type=jnp.float32)


def _allreduce_kernel(groups, nc, fused, *refs):
    if fused:
        a_ref, v_ref, t_ref, o_ref, x_ref, buf1, buf2, red, recv1, recv2, recv3, send_sems, recv_sems = refs
    else:
        x_ref, t_ref, o_ref, buf1, buf2, red, recv1, recv2, recv3, send_sems, recv_sems = refs
    me = lax.axis_index("row")
    col = lax.axis_index("col")
    g1, g2, g3 = groups
    s1, s2, s3 = 1, g1, g1 * g2
    i1 = lax.rem(me, g1)
    i2 = lax.rem(me // s2, g2)
    i3 = me // s3
    rows, cols = x_ref.shape
    cw = cols // nc
    p1 = rows // g1
    p2 = p1 // g2
    p3 = p2 // g3
    mesh_id = pl.DeviceIdType.MESH

    def part(ref, start, size, c):
        return ref.at[pl.ds(pl.multiple_of(start, size), size), pl.ds(c * cw, cw)]

    barrier = pltpu.get_barrier_semaphore()
    for g, stride, mine in ((g1, s1, i1), (g2, s2, i2), (g3, s3, i3)):

        @pl.loop(1, g)
        def _(s):
            j = lax.rem(mine + s, g)
            pl.semaphore_signal(barrier, inc=1, device_id=(me + (j - mine) * stride, col), device_id_type=mesh_id)

    def project(c):
        if fused:
            x_ref[:, pl.ds(c * cw, cw)] = lax.dot_general(
                a_ref[...], v_ref[:, pl.ds(c * cw, cw)], (((0,), (0,)), ((), ())),
                precision=lax.Precision.HIGH, preferred_element_type=jnp.float32,
            )

    project(0)
    pl.semaphore_wait(barrier, g1 + g2 + g3 - 3)

    def exchange(stage, c, g, stride, mine, src_of, dst_of):
        def copy(s):
            j = lax.rem(mine + s, g)
            return pltpu.make_async_remote_copy(
                src_ref=src_of(j),
                dst_ref=dst_of(j, s),
                send_sem=send_sems.at[stage, c, s],
                recv_sem=recv_sems.at[stage, c, s],
                device_id=(me + (j - mine) * stride, col),
                device_id_type=mesh_id,
            )

        def start():
            @pl.loop(1, g)
            def _(s):
                copy(s).start()

        def finish():
            @pl.loop(1, g)
            def _(s):
                copy(s).wait()

        return start, finish

    reduce_plan = (
        (0, g1, s1, i1, x_ref, p1, recv1, buf1),
        (1, g2, s2, i2, buf1, p2, recv2, buf2),
        (2, g3, s3, i3, buf2, p3, recv3, red),
    )

    def reduce_stage(stage, g, stride, mine, src, piece, recv, dst, c):
        start, finish = exchange(
            stage, c, g, stride, mine,
            lambda j: part(src, j * piece, piece, c),
            lambda j, s: recv.at[s, :, pl.ds(c * cw, cw)],
        )

        def combine():
            finish()
            own = src[pl.ds(pl.multiple_of(mine * piece, piece), piece), pl.ds(c * cw, cw)]
            dst[:, pl.ds(c * cw, cw)] = lax.fori_loop(1, g, lambda s, acc: acc + recv[s, :, pl.ds(c * cw, cw)], own)

        return start, combine

    def run(plan, before=lambda c: None):
        for c in range(nc):
            before(c)
            plan[0](c)[0]()
        for k in range(len(plan)):
            for c in range(nc):
                plan[k](c)[1]()
                if k + 1 < len(plan):
                    plan[k + 1](c)[0]()

    run([functools.partial(reduce_stage, *p) for p in reduce_plan], before=lambda c: project(c) if c > 0 else None)

    base3 = i1 * p1 + i2 * p2
    o_ref[pl.ds(pl.multiple_of(base3 + i3 * p3, p3), p3), :] = lax.dot_general(
        t_ref[...], red[...], (((1,), (1,)), ((), ())), precision=lax.Precision.HIGHEST, preferred_element_type=jnp.float32
    ).T

    def gather_stage(stage, g, stride, mine, base, block, c):
        own = part(o_ref, base + mine * block, block, c)
        return exchange(stage, c, g, stride, mine, lambda j: own, lambda j, s: own)

    run([
        functools.partial(gather_stage, 3, g3, s3, i3, base3, p3),
        functools.partial(gather_stage, 4, g2, s2, i2, i1 * p1, p2),
        functools.partial(gather_stage, 5, g1, s1, i1, 0, p1),
    ])


def row_allreduce_times(x, t, n, collective_id, nc=2, factors=None):
    fused = factors is not None
    if fused:
        a, v = factors
        rows, cols, dtype = a.shape[1], v.shape[1], jnp.float32
        operands = (a, v, t)
    else:
        rows, cols = x.shape
        dtype = x.dtype
        operands = (x, t)
    groups = (2, min(4, n // 2), max(1, n // 8))
    g1, g2, g3 = groups
    p1 = rows // g1
    p2 = p1 // g2
    p3 = p2 // g3
    return pl.pallas_call(
        functools.partial(_allreduce_kernel, groups, nc, fused),
        out_shape=jax.ShapeDtypeStruct((rows, cols), dtype),
        in_specs=[pl.BlockSpec(memory_space=pltpu.VMEM)] * len(operands),
        out_specs=pl.BlockSpec(memory_space=pltpu.VMEM),
        scratch_shapes=([pltpu.VMEM((rows, cols), dtype)] if fused else []) + [
            pltpu.VMEM((p1, cols), dtype),
            pltpu.VMEM((p2, cols), dtype),
            pltpu.VMEM((p3, cols), dtype),
            pltpu.VMEM((g1, p1, cols), dtype),
            pltpu.VMEM((g2, p2, cols), dtype),
            pltpu.VMEM((g3, p3, cols), dtype),
            pltpu.SemaphoreType.DMA((6, nc, max(groups))),
            pltpu.SemaphoreType.DMA((6, nc, max(groups))),
        ],
        compiler_params=pltpu.CompilerParams(has_side_effects=True, collective_id=collective_id),
        cost_estimate=pl.CostEstimate(
            flops=rows * cols * (1 + (2 * a.shape[0] if fused else 0)), transcendentals=0, bytes_accessed=4 * rows * cols * 4
        ),
    )(*operands)


def _col_gather_kernel(n, v_ref, e_ref, o_ref, s_ref, send_sems, recv_sems):
    me = lax.axis_index("col")
    row = lax.axis_index("row")
    rows, w = v_ref.shape
    half = rows // 2
    left, right = lax.rem(me + n - 1, n), lax.rem(me + 1, n)

    def block(j):
        return o_ref.at[:, pl.ds(pl.multiple_of(j * w, w), w)]

    def send(src, dst, k, target):
        return pltpu.make_async_remote_copy(
            src_ref=src,
            dst_ref=dst,
            send_sem=send_sems.at[k],
            recv_sem=recv_sems.at[k],
            device_id=(row, target),
            device_id_type=pl.DeviceIdType.MESH,
        )

    barrier = pltpu.get_barrier_semaphore()
    for target in (left, right):
        pl.semaphore_signal(barrier, inc=1, device_id=(row, target), device_id_type=pl.DeviceIdType.MESH)
    pl.semaphore_wait(barrier, 2)

    def rows(view, lo):
        return view.at[pl.ds(lo, half), :]

    to_right = [send(rows(v_ref, lo), rows(block(me), lo), k, right) for k, lo in ((0, 0), (1, half))]
    to_left = [send(rows(v_ref, lo), rows(block(me), lo), k, left) for k, lo in ((2, half), (3, 0))]
    for a, b in zip(to_right, to_left):
        a.start()
        b.start()
    block(me)[...] = v_ref[...]

    def project(j):
        s_ref[:, pl.ds(pl.multiple_of(j * w, w), w)] = lax.dot_general(
            e_ref[...], block(j)[...], (((0,), (0,)), ((), ())), precision=lax.Precision.HIGH, preferred_element_type=jnp.float32
        )

    project(me)
    to_right[0].wait_recv()
    fwd_right = send(rows(block(left), 0), rows(block(left), 0), 4, right)
    fwd_right.start()
    to_left[0].wait_recv()
    fwd_left = send(rows(block(right), half), rows(block(right), half), 5, left)
    fwd_left.start()
    for cp in to_right + to_left:
        cp.wait_send()
    to_right[1].wait_recv()
    project(left)
    to_left[1].wait_recv()
    project(right)
    fwd_right.wait()
    fwd_left.wait()
    project(lax.rem(me + 2, n))


def col_gather(v, e, n):
    assert n == 4
    rows, w = v.shape
    return pl.pallas_call(
        functools.partial(_col_gather_kernel, n),
        out_shape=(
            jax.ShapeDtypeStruct((rows, w * n), v.dtype),
            jax.ShapeDtypeStruct((e.shape[1], w * n), jnp.float32),
        ),
        in_specs=[pl.BlockSpec(memory_space=pltpu.VMEM)] * 2,
        out_specs=(pl.BlockSpec(memory_space=pltpu.VMEM), pl.BlockSpec(memory_space=pltpu.VMEM)),
        scratch_shapes=[pltpu.SemaphoreType.DMA((6,)), pltpu.SemaphoreType.DMA((6,))],
        compiler_params=pltpu.CompilerParams(has_side_effects=True, collective_id=0),
        cost_estimate=pl.CostEstimate(
            flops=2 * rows * e.shape[1] * w * n, transcendentals=0, bytes_accessed=2 * rows * w * n * 4 + rows * e.shape[1] * 4
        ),
    )(v, e)


def on_device(n_row, n_col, eigen_vectors, panel_first, panel_second, factor_first, factor_second):
    vectors_second, partial_second = col_gather(panel_second, eigen_vectors, n_col)
    vectors_second, panel_first = lax.optimization_barrier((vectors_second, panel_first))
    vectors_first = lax.all_gather(panel_first, "col", axis=1, tiled=True)
    updated = eigen_vectors
    for collective_id, vectors, factor in ((1, vectors_second, factor_second), (2, vectors_first, factor_first)):
        if collective_id == 1:
            applied_t = row_allreduce_times(partial_second, factor, n_row, collective_id)
        else:
            applied_t = row_allreduce_times(None, factor, n_row, collective_id, factors=(updated, vectors))
        updated = updated - lax.dot_general(vectors, applied_t, (((1,), (1,)), ((), ())), precision=lax.Precision.HIGH, preferred_element_type=jnp.float32)
    return updated


def solution(mesh):
    return jax.shard_map(
        functools.partial(on_device, mesh.shape["row"], mesh.shape["col"]),
        mesh=mesh,
        in_specs=(P("row", "col"), P("row", "col"), P("row", "col"), P(), P()),
        out_specs=P("row", "col"),
        check_vma=False,
    )
```

```python
import functools

import jax
import jax.numpy as jnp
from jax import lax
from jax.experimental import pallas as pl
from jax.experimental.pallas import tpu as pltpu
from jax.sharding import PartitionSpec as P


def local_dot(left, right):
    return jnp.dot(left, right, precision=lax.Precision.HIGHEST, preferred_element_type=jnp.float32)


def _allreduce_kernel(groups, nc, fused, *refs):
    if fused:
        e_ref, u_ref, w_ref, v_ref, t_ref, o_ref, a_ref, x_ref, buf1, buf2, red, recv1, recv2, recv3, send_sems, recv_sems = refs
    else:
        x_ref, t_ref, o_ref, buf1, buf2, red, recv1, recv2, recv3, send_sems, recv_sems = refs
    me = lax.axis_index("row")
    col = lax.axis_index("col")
    g1, g2, g3 = groups
    s1, s2, s3 = 1, g1, g1 * g2
    i1 = lax.rem(me, g1)
    i2 = lax.rem(me // s2, g2)
    i3 = me // s3
    rows, cols = x_ref.shape
    cw = cols // nc
    p1 = rows // g1
    p2 = p1 // g2
    p3 = p2 // g3
    mesh_id = pl.DeviceIdType.MESH

    def part(ref, start, size, c):
        return ref.at[pl.ds(pl.multiple_of(start, size), size), pl.ds(c * cw, cw)]

    barrier = pltpu.get_barrier_semaphore()
    for g, stride, mine in ((g1, s1, i1), (g2, s2, i2), (g3, s3, i3)):

        @pl.loop(1, g)
        def _(s):
            j = lax.rem(mine + s, g)
            pl.semaphore_signal(barrier, inc=1, device_id=(me + (j - mine) * stride, col), device_id_type=mesh_id)

    def project(c):
        if fused:
            x_ref[:, pl.ds(c * cw, cw)] = lax.dot_general(
                a_ref[...], v_ref[:, pl.ds(c * cw, cw)], (((0,), (0,)), ((), ())),
                precision=lax.Precision.HIGH, preferred_element_type=jnp.float32,
            )

    if fused:
        a_ref[...] = e_ref[...] - lax.dot_general(
            u_ref[...], w_ref[...], (((1,), (1,)), ((), ())), precision=lax.Precision.HIGH, preferred_element_type=jnp.float32
        )
    project(0)
    pl.semaphore_wait(barrier, g1 + g2 + g3 - 3)

    def exchange(stage, c, g, stride, mine, src_of, dst_of):
        def copy(s):
            j = lax.rem(mine + s, g)
            return pltpu.make_async_remote_copy(
                src_ref=src_of(j),
                dst_ref=dst_of(j, s),
                send_sem=send_sems.at[stage, c, s],
                recv_sem=recv_sems.at[stage, c, s],
                device_id=(me + (j - mine) * stride, col),
                device_id_type=mesh_id,
            )

        def start():
            @pl.loop(1, g)
            def _(s):
                copy(s).start()

        def finish():
            @pl.loop(1, g)
            def _(s):
                copy(s).wait()

        return start, finish

    reduce_plan = (
        (0, g1, s1, i1, x_ref, p1, recv1, buf1),
        (1, g2, s2, i2, buf1, p2, recv2, buf2),
        (2, g3, s3, i3, buf2, p3, recv3, red),
    )

    def reduce_stage(stage, g, stride, mine, src, piece, recv, dst, c):
        start, finish = exchange(
            stage, c, g, stride, mine,
            lambda j: part(src, j * piece, piece, c),
            lambda j, s: recv.at[s, :, pl.ds(c * cw, cw)],
        )

        def combine():
            finish()
            own = src[pl.ds(pl.multiple_of(mine * piece, piece), piece), pl.ds(c * cw, cw)]
            dst[:, pl.ds(c * cw, cw)] = lax.fori_loop(1, g, lambda s, acc: acc + recv[s, :, pl.ds(c * cw, cw)], own)

        return start, combine

    def run(plan, before=lambda c: None):
        for c in range(nc):
            before(c)
            plan[0](c)[0]()
        for k in range(len(plan)):
            for c in range(nc):
                plan[k](c)[1]()
                if k + 1 < len(plan):
                    plan[k + 1](c)[0]()

    run([functools.partial(reduce_stage, *p) for p in reduce_plan], before=lambda c: project(c) if c > 0 else None)

    base3 = i1 * p1 + i2 * p2
    o_ref[pl.ds(pl.multiple_of(base3 + i3 * p3, p3), p3), :] = lax.dot_general(
        t_ref[...], red[...], (((1,), (1,)), ((), ())), precision=lax.Precision.HIGHEST, preferred_element_type=jnp.float32
    ).T

    def gather_stage(stage, g, stride, mine, base, block, c):
        own = part(o_ref, base + mine * block, block, c)
        return exchange(stage, c, g, stride, mine, lambda j: own, lambda j, s: own)

    run([
        functools.partial(gather_stage, 3, g3, s3, i3, base3, p3),
        functools.partial(gather_stage, 4, g2, s2, i2, i1 * p1, p2),
        functools.partial(gather_stage, 5, g1, s1, i1, 0, p1),
    ])


def row_allreduce_times(x, t, n, collective_id, nc=2, factors=None):
    fused = factors is not None
    if fused:
        e, u, w, v = factors
        a = e
        rows, cols, dtype = e.shape[1], v.shape[1], jnp.float32
        operands = (e, u, w, v, t)
    else:
        rows, cols = x.shape
        dtype = x.dtype
        operands = (x, t)
    groups = (2, min(4, n // 2), max(1, n // 8))
    g1, g2, g3 = groups
    p1 = rows // g1
    p2 = p1 // g2
    p3 = p2 // g3
    return pl.pallas_call(
        functools.partial(_allreduce_kernel, groups, nc, fused),
        out_shape=(jax.ShapeDtypeStruct((rows, cols), dtype), jax.ShapeDtypeStruct(e.shape, dtype)) if fused else jax.ShapeDtypeStruct((rows, cols), dtype),
        in_specs=[pl.BlockSpec(memory_space=pltpu.VMEM)] * len(operands),
        out_specs=(pl.BlockSpec(memory_space=pltpu.VMEM),) * 2 if fused else pl.BlockSpec(memory_space=pltpu.VMEM),
        scratch_shapes=([pltpu.VMEM((rows, cols), dtype)] if fused else []) + [
            pltpu.VMEM((p1, cols), dtype),
            pltpu.VMEM((p2, cols), dtype),
            pltpu.VMEM((p3, cols), dtype),
            pltpu.VMEM((g1, p1, cols), dtype),
            pltpu.VMEM((g2, p2, cols), dtype),
            pltpu.VMEM((g3, p3, cols), dtype),
            pltpu.SemaphoreType.DMA((6, nc, max(groups))),
            pltpu.SemaphoreType.DMA((6, nc, max(groups))),
        ],
        compiler_params=pltpu.CompilerParams(has_side_effects=True, collective_id=collective_id),
        cost_estimate=pl.CostEstimate(
            flops=rows * cols * (1 + (2 * a.shape[0] if fused else 0)), transcendentals=0, bytes_accessed=4 * rows * cols * 4
        ),
    )(*operands)


def _col_gather_kernel(n, v_ref, e_ref, o_ref, s_ref, send_sems, recv_sems):
    me = lax.axis_index("col")
    row = lax.axis_index("row")
    rows, w = v_ref.shape
    half = rows // 2
    left, right = lax.rem(me + n - 1, n), lax.rem(me + 1, n)

    def block(j):
        return o_ref.at[:, pl.ds(pl.multiple_of(j * w, w), w)]

    def send(src, dst, k, target):
        return pltpu.make_async_remote_copy(
            src_ref=src,
            dst_ref=dst,
            send_sem=send_sems.at[k],
            recv_sem=recv_sems.at[k],
            device_id=(row, target),
            device_id_type=pl.DeviceIdType.MESH,
        )

    barrier = pltpu.get_barrier_semaphore()
    for target in (left, right):
        pl.semaphore_signal(barrier, inc=1, device_id=(row, target), device_id_type=pl.DeviceIdType.MESH)
    pl.semaphore_wait(barrier, 2)

    def rows(view, lo):
        return view.at[pl.ds(lo, half), :]

    to_right = [send(rows(v_ref, lo), rows(block(me), lo), k, right) for k, lo in ((0, 0), (1, half))]
    to_left = [send(rows(v_ref, lo), rows(block(me), lo), k, left) for k, lo in ((2, half), (3, 0))]
    for a, b in zip(to_right, to_left):
        a.start()
        b.start()
    block(me)[...] = v_ref[...]

    def project(j):
        s_ref[:, pl.ds(pl.multiple_of(j * w, w), w)] = lax.dot_general(
            e_ref[...], block(j)[...], (((0,), (0,)), ((), ())), precision=lax.Precision.HIGH, preferred_element_type=jnp.float32
        )

    project(me)
    to_right[0].wait_recv()
    fwd_right = send(rows(block(left), 0), rows(block(left), 0), 4, right)
    fwd_right.start()
    to_left[0].wait_recv()
    fwd_left = send(rows(block(right), half), rows(block(right), half), 5, left)
    fwd_left.start()
    for cp in to_right + to_left:
        cp.wait_send()
    to_right[1].wait_recv()
    project(left)
    to_left[1].wait_recv()
    project(right)
    fwd_right.wait()
    fwd_left.wait()
    project(lax.rem(me + 2, n))


def col_gather(v, e, n):
    assert n == 4
    rows, w = v.shape
    return pl.pallas_call(
        functools.partial(_col_gather_kernel, n),
        out_shape=(
            jax.ShapeDtypeStruct((rows, w * n), v.dtype),
            jax.ShapeDtypeStruct((e.shape[1], w * n), jnp.float32),
        ),
        in_specs=[pl.BlockSpec(memory_space=pltpu.VMEM)] * 2,
        out_specs=(pl.BlockSpec(memory_space=pltpu.VMEM), pl.BlockSpec(memory_space=pltpu.VMEM)),
        scratch_shapes=[pltpu.SemaphoreType.DMA((6,)), pltpu.SemaphoreType.DMA((6,))],
        compiler_params=pltpu.CompilerParams(has_side_effects=True, collective_id=0),
        cost_estimate=pl.CostEstimate(
            flops=2 * rows * e.shape[1] * w * n, transcendentals=0, bytes_accessed=2 * rows * w * n * 4 + rows * e.shape[1] * 4
        ),
    )(v, e)


def on_device(n_row, n_col, eigen_vectors, panel_first, panel_second, factor_first, factor_second):
    vectors_second, partial_second = col_gather(panel_second, eigen_vectors, n_col)
    vectors_second, panel_first = lax.optimization_barrier((vectors_second, panel_first))
    vectors_first = lax.all_gather(panel_first, "col", axis=1, tiled=True)
    applied_second = row_allreduce_times(partial_second, factor_second, n_row, 1)
    applied_first, updated = row_allreduce_times(
        None, factor_first, n_row, 2, factors=(eigen_vectors, vectors_second, applied_second, vectors_first)
    )
    updated = updated - lax.dot_general(vectors_first, applied_first, (((1,), (1,)), ((), ())), precision=lax.Precision.HIGH, preferred_element_type=jnp.float32)
    return updated


def solution(mesh):
    return jax.shard_map(
        functools.partial(on_device, mesh.shape["row"], mesh.shape["col"]),
        mesh=mesh,
        in_specs=(P("row", "col"), P("row", "col"), P("row", "col"), P(), P()),
        out_specs=P("row", "col"),
        check_vma=False,
    )
```

```python
import functools

import jax
import jax.numpy as jnp
from jax import lax
from jax.experimental import pallas as pl
from jax.experimental.pallas import tpu as pltpu
from jax.sharding import PartitionSpec as P


def local_dot(left, right):
    return jnp.dot(left, right, precision=lax.Precision.HIGHEST, preferred_element_type=jnp.float32)


def _allreduce_kernel(groups, nc, fused, *refs):
    if fused:
        e_ref, u_ref, w_ref, v_ref, t_ref, out_ref, o_ref, a_ref, x_ref, buf1, buf2, red, recv1, recv2, recv3, send_sems, recv_sems = refs
    else:
        x_ref, t_ref, o_ref, buf1, buf2, red, recv1, recv2, recv3, send_sems, recv_sems = refs
    me = lax.axis_index("row")
    col = lax.axis_index("col")
    g1, g2, g3 = groups
    s1, s2, s3 = 1, g1, g1 * g2
    i1 = lax.rem(me, g1)
    i2 = lax.rem(me // s2, g2)
    i3 = me // s3
    rows, cols = x_ref.shape
    cw = cols // nc
    p1 = rows // g1
    p2 = p1 // g2
    p3 = p2 // g3
    mesh_id = pl.DeviceIdType.MESH

    def part(ref, start, size, c):
        return ref.at[pl.ds(pl.multiple_of(start, size), size), pl.ds(c * cw, cw)]

    barrier = pltpu.get_barrier_semaphore()
    for g, stride, mine in ((g1, s1, i1), (g2, s2, i2), (g3, s3, i3)):

        @pl.loop(1, g)
        def _(s):
            j = lax.rem(mine + s, g)
            pl.semaphore_signal(barrier, inc=1, device_id=(me + (j - mine) * stride, col), device_id_type=mesh_id)

    def project(c):
        if fused:
            x_ref[:, pl.ds(c * cw, cw)] = lax.dot_general(
                a_ref[...], v_ref[:, pl.ds(c * cw, cw)], (((0,), (0,)), ((), ())),
                precision=lax.Precision.HIGH, preferred_element_type=jnp.float32,
            )

    if fused:
        a_ref[...] = e_ref[...] - lax.dot_general(
            u_ref[...], w_ref[...], (((1,), (1,)), ((), ())), precision=lax.Precision.HIGH, preferred_element_type=jnp.float32
        )
    project(0)
    pl.semaphore_wait(barrier, g1 + g2 + g3 - 3)

    def exchange(stage, c, g, stride, mine, src_of, dst_of):
        def copy(s):
            j = lax.rem(mine + s, g)
            return pltpu.make_async_remote_copy(
                src_ref=src_of(j),
                dst_ref=dst_of(j, s),
                send_sem=send_sems.at[stage, c, s],
                recv_sem=recv_sems.at[stage, c, s],
                device_id=(me + (j - mine) * stride, col),
                device_id_type=mesh_id,
            )

        def start():
            @pl.loop(1, g)
            def _(s):
                copy(s).start()

        def finish():
            @pl.loop(1, g)
            def _(s):
                copy(s).wait()

        return start, finish

    reduce_plan = (
        (0, g1, s1, i1, x_ref, p1, recv1, buf1),
        (1, g2, s2, i2, buf1, p2, recv2, buf2),
        (2, g3, s3, i3, buf2, p3, recv3, red),
    )

    def reduce_stage(stage, g, stride, mine, src, piece, recv, dst, c):
        start, finish = exchange(
            stage, c, g, stride, mine,
            lambda j: part(src, j * piece, piece, c),
            lambda j, s: recv.at[s, :, pl.ds(c * cw, cw)],
        )

        def combine():
            finish()
            own = src[pl.ds(pl.multiple_of(mine * piece, piece), piece), pl.ds(c * cw, cw)]
            dst[:, pl.ds(c * cw, cw)] = lax.fori_loop(1, g, lambda s, acc: acc + recv[s, :, pl.ds(c * cw, cw)], own)

        return start, combine

    def run(plan, before=lambda c: None, last=lambda: None):
        for c in range(nc):
            before(c)
            plan[0](c)[0]()
        for k in range(len(plan)):
            if k == len(plan) - 1:
                last()
            for c in range(nc):
                plan[k](c)[1]()
                if k + 1 < len(plan):
                    plan[k + 1](c)[0]()

    run([functools.partial(reduce_stage, *p) for p in reduce_plan], before=lambda c: project(c) if c > 0 else None)

    base3 = i1 * p1 + i2 * p2
    o_ref[pl.ds(pl.multiple_of(base3 + i3 * p3, p3), p3), :] = lax.dot_general(
        t_ref[...], red[...], (((1,), (1,)), ((), ())), precision=lax.Precision.HIGHEST, preferred_element_type=jnp.float32
    ).T

    def gather_stage(stage, g, stride, mine, base, block, c):
        own = part(o_ref, base + mine * block, block, c)
        return exchange(stage, c, g, stride, mine, lambda j: own, lambda j, s: own)

    def update(half):
        if fused:
            out_ref[:, pl.ds(pl.multiple_of(half * p1, p1), p1)] = a_ref[:, pl.ds(pl.multiple_of(half * p1, p1), p1)] - lax.dot_general(
                v_ref[...], o_ref[pl.ds(pl.multiple_of(half * p1, p1), p1), :], (((1,), (1,)), ((), ())),
                precision=lax.Precision.HIGH, preferred_element_type=jnp.float32,
            )

    run([
        functools.partial(gather_stage, 3, g3, s3, i3, base3, p3),
        functools.partial(gather_stage, 4, g2, s2, i2, i1 * p1, p2),
        functools.partial(gather_stage, 5, g1, s1, i1, 0, p1),
    ], last=lambda: update(i1))
    if g1 == 2:
        update(1 - i1)


def row_allreduce_times(x, t, n, collective_id, nc=2, factors=None):
    fused = factors is not None
    if fused:
        e, u, w, v = factors
        a = e
        rows, cols, dtype = e.shape[1], v.shape[1], jnp.float32
        operands = (e, u, w, v, t)
    else:
        rows, cols = x.shape
        dtype = x.dtype
        operands = (x, t)
    groups = (2, min(4, n // 2), max(1, n // 8))
    g1, g2, g3 = groups
    p1 = rows // g1
    p2 = p1 // g2
    p3 = p2 // g3
    return pl.pallas_call(
        functools.partial(_allreduce_kernel, groups, nc, fused),
        out_shape=jax.ShapeDtypeStruct(e.shape, dtype) if fused else jax.ShapeDtypeStruct((rows, cols), dtype),
        in_specs=[pl.BlockSpec(memory_space=pltpu.VMEM)] * len(operands),
        out_specs=pl.BlockSpec(memory_space=pltpu.VMEM),
        scratch_shapes=([pltpu.VMEM((rows, cols), dtype), pltpu.VMEM(e.shape, dtype), pltpu.VMEM((rows, cols), dtype)] if fused else []) + [
            pltpu.VMEM((p1, cols), dtype),
            pltpu.VMEM((p2, cols), dtype),
            pltpu.VMEM((p3, cols), dtype),
            pltpu.VMEM((g1, p1, cols), dtype),
            pltpu.VMEM((g2, p2, cols), dtype),
            pltpu.VMEM((g3, p3, cols), dtype),
            pltpu.SemaphoreType.DMA((6, nc, max(groups))),
            pltpu.SemaphoreType.DMA((6, nc, max(groups))),
        ],
        compiler_params=pltpu.CompilerParams(has_side_effects=True, collective_id=collective_id),
        cost_estimate=pl.CostEstimate(
            flops=rows * cols * (1 + (2 * a.shape[0] if fused else 0)), transcendentals=0, bytes_accessed=4 * rows * cols * 4
        ),
    )(*operands)


def _col_gather_kernel(n, v_ref, e_ref, o_ref, s_ref, send_sems, recv_sems):
    me = lax.axis_index("col")
    row = lax.axis_index("row")
    rows, w = v_ref.shape
    half = rows // 2
    left, right = lax.rem(me + n - 1, n), lax.rem(me + 1, n)

    def block(j):
        return o_ref.at[:, pl.ds(pl.multiple_of(j * w, w), w)]

    def send(src, dst, k, target):
        return pltpu.make_async_remote_copy(
            src_ref=src,
            dst_ref=dst,
            send_sem=send_sems.at[k],
            recv_sem=recv_sems.at[k],
            device_id=(row, target),
            device_id_type=pl.DeviceIdType.MESH,
        )

    barrier = pltpu.get_barrier_semaphore()
    for target in (left, right):
        pl.semaphore_signal(barrier, inc=1, device_id=(row, target), device_id_type=pl.DeviceIdType.MESH)
    pl.semaphore_wait(barrier, 2)

    def rows(view, lo):
        return view.at[pl.ds(lo, half), :]

    to_right = [send(rows(v_ref, lo), rows(block(me), lo), k, right) for k, lo in ((0, 0), (1, half))]
    to_left = [send(rows(v_ref, lo), rows(block(me), lo), k, left) for k, lo in ((2, half), (3, 0))]
    for a, b in zip(to_right, to_left):
        a.start()
        b.start()
    block(me)[...] = v_ref[...]

    def project(j):
        s_ref[:, pl.ds(pl.multiple_of(j * w, w), w)] = lax.dot_general(
            e_ref[...], block(j)[...], (((0,), (0,)), ((), ())), precision=lax.Precision.HIGH, preferred_element_type=jnp.float32
        )

    project(me)
    to_right[0].wait_recv()
    fwd_right = send(rows(block(left), 0), rows(block(left), 0), 4, right)
    fwd_right.start()
    to_left[0].wait_recv()
    fwd_left = send(rows(block(right), half), rows(block(right), half), 5, left)
    fwd_left.start()
    for cp in to_right + to_left:
        cp.wait_send()
    to_right[1].wait_recv()
    project(left)
    to_left[1].wait_recv()
    project(right)
    fwd_right.wait()
    fwd_left.wait()
    project(lax.rem(me + 2, n))


def col_gather(v, e, n):
    assert n == 4
    rows, w = v.shape
    return pl.pallas_call(
        functools.partial(_col_gather_kernel, n),
        out_shape=(
            jax.ShapeDtypeStruct((rows, w * n), v.dtype),
            jax.ShapeDtypeStruct((e.shape[1], w * n), jnp.float32),
        ),
        in_specs=[pl.BlockSpec(memory_space=pltpu.VMEM)] * 2,
        out_specs=(pl.BlockSpec(memory_space=pltpu.VMEM), pl.BlockSpec(memory_space=pltpu.VMEM)),
        scratch_shapes=[pltpu.SemaphoreType.DMA((6,)), pltpu.SemaphoreType.DMA((6,))],
        compiler_params=pltpu.CompilerParams(has_side_effects=True, collective_id=0),
        cost_estimate=pl.CostEstimate(
            flops=2 * rows * e.shape[1] * w * n, transcendentals=0, bytes_accessed=2 * rows * w * n * 4 + rows * e.shape[1] * 4
        ),
    )(v, e)


def on_device(n_row, n_col, eigen_vectors, panel_first, panel_second, factor_first, factor_second):
    vectors_second, partial_second = col_gather(panel_second, eigen_vectors, n_col)
    vectors_second, panel_first = lax.optimization_barrier((vectors_second, panel_first))
    vectors_first = lax.all_gather(panel_first, "col", axis=1, tiled=True)
    applied_second = row_allreduce_times(partial_second, factor_second, n_row, 1)
    updated = row_allreduce_times(
        None, factor_first, n_row, 2, factors=(eigen_vectors, vectors_second, applied_second, vectors_first)
    )
    return updated


def solution(mesh):
    return jax.shard_map(
        functools.partial(on_device, mesh.shape["row"], mesh.shape["col"]),
        mesh=mesh,
        in_specs=(P("row", "col"), P("row", "col"), P("row", "col"), P(), P()),
        out_specs=P("row", "col"),
        check_vma=False,
    )
```

```python
import functools

import jax
import jax.numpy as jnp
from jax import lax
from jax.experimental import pallas as pl
from jax.experimental.pallas import tpu as pltpu
from jax.sharding import PartitionSpec as P


def local_dot(left, right):
    return jnp.dot(left, right, precision=lax.Precision.HIGHEST, preferred_element_type=jnp.float32)


def _allreduce_kernel(groups, nc, fused, *refs):
    if fused:
        e_ref, u_ref, w_ref, v_ref, t_ref, out_ref, o_ref, a_ref, x_ref, buf1, buf2, red, recv1, recv2, recv3, send_sems, recv_sems = refs
    else:
        x_ref, t_ref, o_ref, buf1, buf2, red, recv1, recv2, recv3, send_sems, recv_sems = refs
    me = lax.axis_index("row")
    col = lax.axis_index("col")
    g1, g2, g3 = groups
    s1, s2, s3 = 1, g1, g1 * g2
    i1 = lax.rem(me, g1)
    i2 = lax.rem(me // s2, g2)
    i3 = me // s3
    rows, cols = x_ref.shape
    cw = cols // nc
    p1 = rows // g1
    p2 = p1 // g2
    p3 = p2 // g3
    mesh_id = pl.DeviceIdType.MESH

    def part(ref, start, size, c):
        return ref.at[pl.ds(pl.multiple_of(start, size), size), pl.ds(c * cw, cw)]

    barrier = pltpu.get_barrier_semaphore()
    for g, stride, mine in ((g1, s1, i1), (g2, s2, i2), (g3, s3, i3)):

        @pl.loop(1, g)
        def _(s):
            j = lax.rem(mine + s, g)
            pl.semaphore_signal(barrier, inc=1, device_id=(me + (j - mine) * stride, col), device_id_type=mesh_id)

    def project(c):
        if fused:
            x_ref[:, pl.ds(c * cw, cw)] = lax.dot_general(
                a_ref[...], v_ref[:, pl.ds(c * cw, cw)], (((0,), (0,)), ((), ())),
                precision=lax.Precision.HIGH, preferred_element_type=jnp.float32,
            )

    if fused:
        a_ref[...] = e_ref[...] - lax.dot_general(
            u_ref[...], w_ref[...], (((1,), (1,)), ((), ())), precision=lax.Precision.HIGH, preferred_element_type=jnp.float32
        )
    project(0)
    pl.semaphore_wait(barrier, g1 + g2 + g3 - 3)

    def exchange(stage, c, g, stride, mine, src_of, dst_of):
        def copy(s):
            j = lax.rem(mine + s, g)
            return pltpu.make_async_remote_copy(
                src_ref=src_of(j),
                dst_ref=dst_of(j, s),
                send_sem=send_sems.at[stage, c, s],
                recv_sem=recv_sems.at[stage, c, s],
                device_id=(me + (j - mine) * stride, col),
                device_id_type=mesh_id,
            )

        def start():
            @pl.loop(1, g)
            def _(s):
                copy(s).start()

        def finish():
            @pl.loop(1, g)
            def _(s):
                copy(s).wait()

        return start, finish

    reduce_plan = (
        (0, g1, s1, i1, x_ref, p1, recv1, buf1),
        (1, g2, s2, i2, buf1, p2, recv2, buf2),
        (2, g3, s3, i3, buf2, p3, recv3, red),
    )

    def reduce_stage(stage, g, stride, mine, src, piece, recv, dst, c):
        start, finish = exchange(
            stage, c, g, stride, mine,
            lambda j: part(src, j * piece, piece, c),
            lambda j, s: recv.at[s, :, pl.ds(c * cw, cw)],
        )

        def combine():
            finish()
            own = src[pl.ds(pl.multiple_of(mine * piece, piece), piece), pl.ds(c * cw, cw)]
            dst[:, pl.ds(c * cw, cw)] = lax.fori_loop(1, g, lambda s, acc: acc + recv[s, :, pl.ds(c * cw, cw)], own)

        return start, combine

    def run(plan, before=lambda c: None, last=lambda: None, after=lambda c: None):
        for c in range(nc):
            before(c)
            plan[0](c)[0]()
        for k in range(len(plan)):
            if k == len(plan) - 1:
                last()
            for c in range(nc):
                plan[k](c)[1]()
                if k + 1 < len(plan):
                    plan[k + 1](c)[0]()
                else:
                    after(c)

    run([functools.partial(reduce_stage, *p) for p in reduce_plan], before=lambda c: project(c) if c > 0 else None)

    base3 = i1 * p1 + i2 * p2
    o_ref[pl.ds(pl.multiple_of(base3 + i3 * p3, p3), p3), :] = lax.dot_general(
        t_ref[...], red[...], (((1,), (1,)), ((), ())), precision=lax.Precision.HIGHEST, preferred_element_type=jnp.float32
    ).T

    def gather_stage(stage, g, stride, mine, base, block, c):
        own = part(o_ref, base + mine * block, block, c)
        return exchange(stage, c, g, stride, mine, lambda j: own, lambda j, s: own)

    def update(half):
        if fused:
            out_ref[:, pl.ds(pl.multiple_of(half * p1, p1), p1)] = a_ref[:, pl.ds(pl.multiple_of(half * p1, p1), p1)] - lax.dot_general(
                v_ref[...], o_ref[pl.ds(pl.multiple_of(half * p1, p1), p1), :], (((1,), (1,)), ((), ())),
                precision=lax.Precision.HIGH, preferred_element_type=jnp.float32,
            )

    def update_chunk(half, c):
        if fused and g1 == 2:
            cols_half = pl.ds(pl.multiple_of(half * p1, p1), p1)
            term = lax.dot_general(
                v_ref[:, pl.ds(c * cw, cw)], o_ref[cols_half, pl.ds(c * cw, cw)], (((1,), (1,)), ((), ())),
                precision=lax.Precision.HIGH, preferred_element_type=jnp.float32,
            )
            if c == 0:
                out_ref[:, cols_half] = a_ref[:, cols_half] - term
            else:
                out_ref[:, cols_half] -= term

    run([
        functools.partial(gather_stage, 3, g3, s3, i3, base3, p3),
        functools.partial(gather_stage, 4, g2, s2, i2, i1 * p1, p2),
        functools.partial(gather_stage, 5, g1, s1, i1, 0, p1),
    ], last=lambda: update(i1), after=lambda c: update_chunk(1 - i1, c))


def row_allreduce_times(x, t, n, collective_id, nc=2, factors=None):
    fused = factors is not None
    if fused:
        e, u, w, v = factors
        a = e
        rows, cols, dtype = e.shape[1], v.shape[1], jnp.float32
        operands = (e, u, w, v, t)
    else:
        rows, cols = x.shape
        dtype = x.dtype
        operands = (x, t)
    groups = (2, min(4, n // 2), max(1, n // 8))
    g1, g2, g3 = groups
    p1 = rows // g1
    p2 = p1 // g2
    p3 = p2 // g3
    return pl.pallas_call(
        functools.partial(_allreduce_kernel, groups, nc, fused),
        out_shape=jax.ShapeDtypeStruct(e.shape, dtype) if fused else jax.ShapeDtypeStruct((rows, cols), dtype),
        in_specs=[pl.BlockSpec(memory_space=pltpu.VMEM)] * len(operands),
        out_specs=pl.BlockSpec(memory_space=pltpu.VMEM),
        scratch_shapes=([pltpu.VMEM((rows, cols), dtype), pltpu.VMEM(e.shape, dtype), pltpu.VMEM((rows, cols), dtype)] if fused else []) + [
            pltpu.VMEM((p1, cols), dtype),
            pltpu.VMEM((p2, cols), dtype),
            pltpu.VMEM((p3, cols), dtype),
            pltpu.VMEM((g1, p1, cols), dtype),
            pltpu.VMEM((g2, p2, cols), dtype),
            pltpu.VMEM((g3, p3, cols), dtype),
            pltpu.SemaphoreType.DMA((6, nc, max(groups))),
            pltpu.SemaphoreType.DMA((6, nc, max(groups))),
        ],
        compiler_params=pltpu.CompilerParams(has_side_effects=True, collective_id=collective_id),
        cost_estimate=pl.CostEstimate(
            flops=rows * cols * (1 + (2 * a.shape[0] if fused else 0)), transcendentals=0, bytes_accessed=4 * rows * cols * 4
        ),
    )(*operands)


def _col_gather_kernel(n, v_ref, e_ref, o_ref, s_ref, send_sems, recv_sems):
    me = lax.axis_index("col")
    row = lax.axis_index("row")
    rows, w = v_ref.shape
    half = rows // 2
    left, right = lax.rem(me + n - 1, n), lax.rem(me + 1, n)

    def block(j):
        return o_ref.at[:, pl.ds(pl.multiple_of(j * w, w), w)]

    def send(src, dst, k, target):
        return pltpu.make_async_remote_copy(
            src_ref=src,
            dst_ref=dst,
            send_sem=send_sems.at[k],
            recv_sem=recv_sems.at[k],
            device_id=(row, target),
            device_id_type=pl.DeviceIdType.MESH,
        )

    barrier = pltpu.get_barrier_semaphore()
    for target in (left, right):
        pl.semaphore_signal(barrier, inc=1, device_id=(row, target), device_id_type=pl.DeviceIdType.MESH)
    pl.semaphore_wait(barrier, 2)

    def rows(view, lo):
        return view.at[pl.ds(lo, half), :]

    to_right = [send(rows(v_ref, lo), rows(block(me), lo), k, right) for k, lo in ((0, 0), (1, half))]
    to_left = [send(rows(v_ref, lo), rows(block(me), lo), k, left) for k, lo in ((2, half), (3, 0))]
    for a, b in zip(to_right, to_left):
        a.start()
        b.start()
    block(me)[...] = v_ref[...]

    def project(j):
        s_ref[:, pl.ds(pl.multiple_of(j * w, w), w)] = lax.dot_general(
            e_ref[...], block(j)[...], (((0,), (0,)), ((), ())), precision=lax.Precision.HIGH, preferred_element_type=jnp.float32
        )

    project(me)
    to_right[0].wait_recv()
    fwd_right = send(rows(block(left), 0), rows(block(left), 0), 4, right)
    fwd_right.start()
    to_left[0].wait_recv()
    fwd_left = send(rows(block(right), half), rows(block(right), half), 5, left)
    fwd_left.start()
    for cp in to_right + to_left:
        cp.wait_send()
    to_right[1].wait_recv()
    project(left)
    to_left[1].wait_recv()
    project(right)
    fwd_right.wait()
    fwd_left.wait()
    project(lax.rem(me + 2, n))


def col_gather(v, e, n):
    assert n == 4
    rows, w = v.shape
    return pl.pallas_call(
        functools.partial(_col_gather_kernel, n),
        out_shape=(
            jax.ShapeDtypeStruct((rows, w * n), v.dtype),
            jax.ShapeDtypeStruct((e.shape[1], w * n), jnp.float32),
        ),
        in_specs=[pl.BlockSpec(memory_space=pltpu.VMEM)] * 2,
        out_specs=(pl.BlockSpec(memory_space=pltpu.VMEM), pl.BlockSpec(memory_space=pltpu.VMEM)),
        scratch_shapes=[pltpu.SemaphoreType.DMA((6,)), pltpu.SemaphoreType.DMA((6,))],
        compiler_params=pltpu.CompilerParams(has_side_effects=True, collective_id=0),
        cost_estimate=pl.CostEstimate(
            flops=2 * rows * e.shape[1] * w * n, transcendentals=0, bytes_accessed=2 * rows * w * n * 4 + rows * e.shape[1] * 4
        ),
    )(v, e)


def on_device(n_row, n_col, eigen_vectors, panel_first, panel_second, factor_first, factor_second):
    vectors_second, partial_second = col_gather(panel_second, eigen_vectors, n_col)
    vectors_second, panel_first = lax.optimization_barrier((vectors_second, panel_first))
    vectors_first = lax.all_gather(panel_first, "col", axis=1, tiled=True)
    applied_second = row_allreduce_times(partial_second, factor_second, n_row, 1)
    updated = row_allreduce_times(
        None, factor_first, n_row, 2, factors=(eigen_vectors, vectors_second, applied_second, vectors_first)
    )
    return updated


def solution(mesh):
    return jax.shard_map(
        functools.partial(on_device, mesh.shape["row"], mesh.shape["col"]),
        mesh=mesh,
        in_specs=(P("row", "col"), P("row", "col"), P("row", "col"), P(), P()),
        out_specs=P("row", "col"),
        check_vma=False,
    )
```
